32 devices in a mesh: block: 8 (over z, x), tm: 4 (over y, core).
Axes of the slice: x: 2, y: 2, z: 4, core: 2. Of those that a mesh axis runs over, the one named last changes fastest.
Arguments:
- traces: float32 [256, 8192], P('block', 'tm'), may hold values from -600 to 600, as said below
- partners: int32 [2, 8], replicated, may hold values from 0 to 7, as said below
- slab_lengths: int32 [4], replicated, may hold values from 1024 to 2048, as said below
Outputs:
- correlations: float32 [256, 101, 3, 32], P(('block', 'tm'))
The draws below stay inside these ranges and needn't reach their ends.
Inputs may be any that keep to these rules, and one draw needn't show every extreme that they name: partners[r, b] = b XOR m_r, where m_r is a nonzero number below 8, the same for every block and different in every round; one of the rounds has m_r = 4. `slab_lengths`: some slab is complete and some slab holds exactly 1024 recorded samples. `traces`: real values.
All inputs are finite; a program needn't handle non-finite values.
Results may differ from the reference program's by a relative error of at most 0.0041.
Values may be sent and summed in bfloat16 or wider, within the bound.
A program may use at most 64 MiB of HBM per device.

```python
import math
import jax
import jax.numpy as jnp
from jax import lax

CB = 32
HALF = 50
ROUNDS = 2
SLAB = 2048
LAGS = 101
CH = 256
SLABS = 4
SAMPLES = 8192
N_BLOCK = 8


def draw_traces(key, part):
    first, second = jax.random.split(key)
    timeline = jnp.arange(SAMPLES, dtype=jnp.float32) / SAMPLES
    base = jnp.clip(jax.random.normal(first, (CH, SAMPLES), jnp.float32), -6.0, 6.0)
    scales = jnp.exp(jax.random.uniform(second, (CH, 1), jnp.float32, 0.0, math.log(10.0)))
    envelope = jnp.exp(timeline * math.log(10.0))
    return (base * scales * envelope[None, :]).astype(jnp.float32)


def draw_partners(key, part):
    half_mask = jnp.int32(N_BLOCK // 2)
    other = jax.random.randint(jax.random.fold_in(key, 11), (), 1, N_BLOCK - 1, dtype=jnp.int32)
    other = jnp.where(other >= half_mask, other + 1, other).astype(jnp.int32)
    flip = jax.random.randint(jax.random.fold_in(key, 12), (), 0, 2, dtype=jnp.int32)
    first_mask = jnp.where(flip == 1, other, half_mask).astype(jnp.int32)
    second_mask = jnp.where(flip == 1, half_mask, other).astype(jnp.int32)
    masks = jnp.stack([first_mask, second_mask]).astype(jnp.int32)
    labels = jnp.arange(N_BLOCK, dtype=jnp.int32)
    return jnp.bitwise_xor(labels[None, :], masks[:, None]).astype(jnp.int32)


def draw_slab_lengths(key, part):
    first = jax.random.fold_in(key, 21)
    second = jax.random.fold_in(key, 22)
    lengths = jax.random.randint(first, (SLABS,), SLAB // 2, SLAB + 1, dtype=jnp.int32)
    order = jax.random.permutation(second, SLABS)
    lengths = lengths.at[order[0]].set(SLAB)
    lengths = lengths.at[order[1]].set(SLAB // 2)
    return lengths.astype(jnp.int32)


def setup_inputs(seed: int = 0) -> dict:
    streams_of = jax.random.split(jax.random.key(seed), 4)
    traces = draw_traces(jax.random.fold_in(streams_of[3], 71), 0)
    partners = draw_partners(jax.random.fold_in(streams_of[3], 71), 0)
    slab_lengths = draw_slab_lengths(jax.random.fold_in(streams_of[3], 71), 0)
    return {"traces": traces, "partners": partners, "slab_lengths": slab_lengths}


def reference(traces, partners, slab_lengths):
    position = jnp.arange(SAMPLES, dtype=jnp.int32)
    slab = position // SLAB
    within = position % SLAB
    length = slab_lengths[slab]
    begin = length // 2
    missing = SLAB - length
    recorded = (within < begin) | (within >= begin + missing)
    gapped = jnp.where(recorded[None, :], traces, jnp.float32(0.0))
    count = jnp.sum(slab_lengths).astype(jnp.float32)
    power = lax.optimization_barrier(jnp.sum(gapped * gapped, axis=1)) / count + 1e-06
    whitened = (gapped / jnp.sqrt(power)[:, None]).astype(jnp.bfloat16)
    whole = whitened.astype(jnp.float32)
    padded = jnp.pad(whole, ((0, 0), (HALF, HALF)))
    zero = jnp.int32(0)

    def per_block(index):
        own = lax.dynamic_slice(padded, ((index * CB).astype(jnp.int32), zero), (CB, SAMPLES + 2 * HALF))
        pieces = [lax.dynamic_slice(whole, ((index * CB).astype(jnp.int32), zero), (CB, SAMPLES))]
        for turn in range(ROUNDS):
            target = partners[turn, index]
            pieces.append(lax.dynamic_slice(whole, ((target * CB).astype(jnp.int32), zero), (CB, SAMPLES)))
        others = jnp.concatenate(pieces, axis=0)

        def per_lag(lag_index):
            shifted = lax.dynamic_slice(own, (zero, (2 * HALF - lag_index).astype(jnp.int32)), (CB, SAMPLES))
            return jnp.dot(shifted, others.T, preferred_element_type=jnp.float32)
        return lax.map(per_lag, jnp.arange(LAGS, dtype=jnp.int32))
    result = lax.map(per_block, jnp.arange(N_BLOCK, dtype=jnp.int32))
    result = result.reshape(N_BLOCK, LAGS, CB, ROUNDS + 1, CB)
    result = jnp.transpose(result, (0, 2, 1, 3, 4)).reshape(CH, LAGS, ROUNDS + 1, CB)
    result = result * (1.0 / jnp.sqrt(count))
    row_in_block = jnp.arange(CH, dtype=jnp.int32) % CB
    column = jnp.arange(CB, dtype=jnp.int32)
    lag_axis = jnp.arange(LAGS, dtype=jnp.int32)
    kind_axis = jnp.arange(ROUNDS + 1, dtype=jnp.int32)
    killed = (row_in_block[:, None, None, None] == column[None, None, None, :]) & (lag_axis[None, :, None, None] == HALF) & (kind_axis[None, None, :, None] == 0)
    return jnp.where(killed, jnp.float32(0.0), result)
```

```python
import functools

import jax
import jax.numpy as jnp
from jax import lax
from jax.experimental import pallas as pl
from jax.experimental.pallas import tpu as pltpu
from jax.sharding import PartitionSpec as P

HALF = 50
ROUNDS = 2
LAGS = 101
FINE = 8
COARSE = 13
PAD = 128
CHUNKS = 8
STOPS = (3, 5, 6, 7)
MESH = pl.DeviceIdType.MESH


def routes(nb):
    bits = nb.bit_length() - 2
    return [(low, min(4, 2 << (bits - 1 - low))) for low in range(0, bits, 2)]


def kernel(
    nb, nt, rows, width,
    traces_ref, partners_ref, lengths_ref, out_ref,
    raw, edge, esend, erecv, ext, lhs, rhs, padded, cross, hops, norms, part, parts,
    load_sem, esend_sem, erecv_sem, hsend_sem, hrecv_sem,
    csend_sem, crecv_sem, bsend_sem, brecv_sem,
    nsend_sem, nrecv_sem, psend_sem, precv_sem,
):
    b = lax.axis_index("block")
    t = lax.axis_index("tm")
    half_mask = nb // 2
    share = rows // nt
    chunk = width // CHUNKS
    span = width + PAD
    f32, bf16 = jnp.float32, jnp.bfloat16

    def at_tm(i):
        return (b, lax.rem(t + i, nt))

    def flip(mask):
        target = b
        for i in range(nb.bit_length() - 1):
            if mask >> i & 1:
                size = 2 << i
                low = lax.rem(target, size)
                target = target - low + lax.rem(low + (1 << i), size)
        return (target, t)

    digits = routes(nb)

    barrier = pltpu.get_barrier_semaphore()
    load = pltpu.make_async_copy(traces_ref, raw, load_sem)
    load.start()
    peers = [at_tm(i) for i in range(1, nt)] + [flip(half_mask)]
    peers += [flip(m << low) for low, ways in digits for m in range(1, ways)]
    for peer in peers:
        pl.semaphore_signal(barrier, inc=1, device_id=peer, device_id_type=MESH)

    def gap(values, index, first):
        length = lengths_ref[index]
        begin = length // 2
        position = first + lax.broadcasted_iota(jnp.int32, values.shape, 1)
        recorded = (position < begin) | (position >= begin + width - length)
        return jnp.where(recorded, values, 0.0)

    load.wait()
    total = jnp.zeros((rows, PAD), f32)
    for ch in range(CHUNKS):
        piece = gap(raw[:, ch * chunk : (ch + 1) * chunk], t, ch * chunk)
        cross[0, ch] = piece.astype(bf16)
        for i in range(chunk // PAD):
            tile = piece[:, i * PAD : (i + 1) * PAD]
            total = total + tile * tile
    esend[...] = total
    pl.semaphore_wait(barrier, len(peers))

    energy = []
    for i in range(1, nt):
        copy = pltpu.make_async_remote_copy(
            esend, erecv.at[i], esend_sem.at[i], erecv_sem.at[i],
            device_id=at_tm(i), device_id_type=MESH,
        )
        copy.start()
        energy.append(copy)
    to_next = pltpu.make_async_remote_copy(
        raw.at[:, pl.ds(width - PAD, PAD)], edge.at[0], hsend_sem.at[0], hrecv_sem.at[0],
        device_id=at_tm(1), device_id_type=MESH,
    )
    to_previous = pltpu.make_async_remote_copy(
        raw.at[:, pl.ds(0, PAD)], edge.at[1], hsend_sem.at[1], hrecv_sem.at[1],
        device_id=at_tm(nt - 1), device_id_type=MESH,
    )
    to_next.start()
    to_previous.start()
    crossing = []
    for ch in range(CHUNKS):
        copy = pltpu.make_async_remote_copy(
            cross.at[0, ch], cross.at[1, ch], csend_sem.at[ch], crecv_sem.at[ch],
            device_id=flip(half_mask), device_id_type=MESH,
        )
        copy.start()
        crossing.append(copy)

    summed = lengths_ref[0]
    for i in range(1, nt):
        summed = summed + lengths_ref[i]
    count = jnp.full((1, 1), summed, jnp.int32).astype(f32)
    padded[:, :PAD] = jnp.zeros((rows, PAD), bf16)
    padded[:, PAD + width :] = jnp.zeros((rows, PAD), bf16)

    for copy in energy:
        copy.wait_recv()
    for i in range(1, nt):
        total = total + erecv[i]
    power = jnp.sum(total, axis=1, keepdims=True) / count + 1e-06
    root = jnp.sqrt(power)

    def whiten(values):
        return (values / root).astype(bf16)

    norms[0, 0] = jnp.broadcast_to(1.0 / root, (rows, PAD))

    def pass_norm(stage, masks):
        copies = []
        for i, mask in enumerate(masks):
            copy = pltpu.make_async_remote_copy(
                norms.at[stage, 0], norms.at[stage, 1 + i],
                nsend_sem.at[stage, i], nrecv_sem.at[stage, i],
                device_id=flip(mask), device_id_type=MESH,
            )
            copy.start()
            copies.append(copy)
        return copies

    normed = [pass_norm(0, [half_mask])]
    for ch in range(CHUNKS):
        piece = whiten(gap(raw[:, ch * chunk : (ch + 1) * chunk], t, ch * chunk))
        ext[:, PAD + ch * chunk : PAD + (ch + 1) * chunk] = piece.astype(f32)
        padded[:, PAD + ch * chunk : PAD + (ch + 1) * chunk] = piece

    to_next.wait_recv()
    to_previous.wait_recv()
    before = whiten(gap(edge[0], lax.rem(t + nt - 1, nt), width - PAD)).astype(f32)
    after = whiten(gap(edge[1], lax.rem(t + 1, nt), 0)).astype(f32)
    ext[:, :PAD] = jnp.where(t > 0, before, 0.0)
    ext[:, PAD + width :] = jnp.where(t < nt - 1, after, 0.0)

    top = FINE * (COARSE - 1) - HALF
    for pair in range(rows // 2):
        both = []
        for c in (2 * pair, 2 * pair + 1):
            row = jnp.broadcast_to(ext[c : c + 1, :], (FINE, width + 2 * PAD))
            rolled = pltpu.roll(
                row, width + 2 * PAD - (PAD - top), 1, stride=1, stride_axis=0
            )
            both.append(rolled[:, :span])
        lhs[2 * FINE * pair : 2 * FINE * (pair + 1), :] = jnp.concatenate(both, axis=0).astype(bf16)

    sends = []

    def multiply(first, last):
        for a in range(COARSE):
            offset = PAD - FINE * (COARSE - 1) + FINE * a
            rhs[a * rows : (a + 1) * rows, first:last] = padded[:, offset + first : offset + last]
        return lax.dot_general(
            lhs[:, first:last], rhs[:, first:last],
            (((1,), (1,)), ((), ())), preferred_element_type=f32,
        )

    def scatter(slot, product):
        part[slot] = product.astype(bf16).reshape(nt, share * FINE, COARSE * rows)
        for i in range(1, nt):
            copy = pltpu.make_async_remote_copy(
                part.at[slot, lax.rem(t + i, nt)], parts.at[slot, i],
                psend_sem.at[slot, i], precv_sem.at[slot, i],
                device_id=at_tm(i), device_id_type=MESH,
            )
            copy.start()
            sends.append(copy)

    scatter(0, multiply(0, span))

    first_mask = partners_ref[0, 0]
    second_mask = partners_ref[1, 0]
    swapped = first_mask != half_mask
    other = jnp.where(swapped, first_mask, second_mask)
    crossed = other >= half_mask

    hop_copies = []
    arrivals = {}

    def forward(stage, ch, piece):
        low, ways = digits[stage]
        hops[stage, 0, ch] = piece
        for m in range(ways - 1, 0, -1):
            copy = pltpu.make_async_remote_copy(
                hops.at[stage, 0, ch], hops.at[stage, m, ch],
                bsend_sem.at[stage, m, ch], brecv_sem.at[stage, m, ch],
                device_id=flip(m << low), device_id_type=MESH,
            )
            copy.start()
            hop_copies.append(copy)
            arrivals[stage, m, ch] = copy

    def choose(stage, choices):
        low, ways = digits[stage]
        digit = lax.rem(other // (1 << low), ways)
        piece = choices[0]
        for m in range(1, ways):
            piece = jnp.where(digit == m, choices[m], piece)
        return piece

    def place(ch, piece):
        padded[:, PAD + ch * chunk : PAD + (ch + 1) * chunk] = piece

    def through(ch):
        edge = (ch + 1) * chunk
        return span if ch == CHUNKS - 1 else edge

    for ch in range(CHUNKS):
        crossing[ch].wait_recv()
        arrived = cross[1, ch]
        forward(0, ch, jnp.where(crossed, arrived, cross[0, ch]))
        place(ch, arrived)
    scatter(1, multiply(0, span))
    normed[0][0].wait_recv()
    factor = jnp.where(crossed, norms[0, 1], norms[0, 0])
    for stage, (low, ways) in enumerate(digits):
        norms[stage + 1, 0] = factor
        normed.append(pass_norm(stage + 1, [m << low for m in range(1, ways)]))
        total = None
        done = 0
        for ch in range(CHUNKS):
            for m in range(1, ways):
                arrivals[stage, m, ch].wait_recv()
            piece = choose(stage, [hops[stage, m, ch] for m in range(ways)])
            if stage < len(digits) - 1:
                forward(stage + 1, ch, piece)
                continue
            place(ch, piece)
            if ch in STOPS:
                product = multiply(done, through(ch))
                total = product if total is None else total + product
                done = through(ch)
        if stage == len(digits) - 1:
            scatter(2, total)
        for copy in normed[stage + 1]:
            copy.wait_recv()
        factor = choose(stage, [norms[stage + 1, m] for m in range(ways)])

    scale = 1.0 / jnp.sqrt(count)
    results = []
    for slot in range(ROUNDS + 1):
        mine = part[slot, t].astype(f32)
        for i in range(1, nt):
            sends[slot * (nt - 1) + i - 1].wait_recv()
            mine = mine + parts[slot, i].astype(f32)
        results.append(mine * scale)
    ordered = [
        results[0],
        jnp.where(swapped, results[2], results[1]),
        jnp.where(swapped, results[1], results[2]),
    ]
    near = norms[0, 1]
    factors = jnp.concatenate(
        [
            jnp.ones((rows, PAD), f32),
            jnp.where(swapped, factor, near),
            jnp.where(swapped, near, factor),
        ],
        axis=0,
    )
    fine = lax.broadcasted_iota(jnp.int32, (FINE, rows), 0)
    column = lax.broadcasted_iota(jnp.int32, (FINE, rows), 1)
    for c in range(share):
        lags = []
        for a in range(COARSE):
            tiles = [
                x[c * FINE : (c + 1) * FINE, a * rows : (a + 1) * rows] for x in ordered
            ]
            if a == HALF // FINE:
                killed = (fine == HALF % FINE) & (column == t * share + c)
                tiles[0] = jnp.where(killed, 0.0, tiles[0])
            spare = PAD - len(tiles) * rows
            lags.append(jnp.concatenate(tiles + [jnp.zeros((FINE, spare), f32)], axis=1))
        lags.append(jnp.zeros((PAD - FINE * COARSE, PAD), f32))
        turned = jnp.concatenate(lags, axis=0).T
        out_ref[c] = (turned[: len(ordered) * rows] * factors)[:, :LAGS]

    for copy in energy + [to_next, to_previous] + crossing + hop_copies + sum(normed, []) + sends:
        copy.wait_send()


def shards(nb, nt, traces, partners, lengths):
    rows, width = traces.shape
    share = rows // nt
    digits = routes(nb)
    depth = len(digits)
    chunk = width // CHUNKS
    span = width + PAD
    f32, bf16 = jnp.float32, jnp.bfloat16
    dma = pltpu.SemaphoreType.DMA
    slots = ROUNDS + 1
    found = pl.pallas_call(
        functools.partial(kernel, nb, nt, rows, width),
        out_shape=jax.ShapeDtypeStruct((share, slots * rows, LAGS), f32),
        in_specs=[
            pl.BlockSpec(memory_space=pl.ANY),
            pl.BlockSpec(memory_space=pltpu.SMEM),
            pl.BlockSpec(memory_space=pltpu.SMEM),
        ],
        out_specs=pl.BlockSpec(memory_space=pltpu.VMEM),
        scratch_shapes=[
            pltpu.VMEM((rows, width), f32),
            pltpu.VMEM((2, rows, PAD), f32),
            pltpu.VMEM((rows, PAD), f32),
            pltpu.VMEM((nt, rows, PAD), f32),
            pltpu.VMEM((rows, width + 2 * PAD), f32),
            pltpu.VMEM((rows * FINE, span), bf16),
            pltpu.VMEM((COARSE * rows, span), bf16),
            pltpu.VMEM((rows, width + 2 * PAD), bf16),
            pltpu.VMEM((2, CHUNKS, rows, chunk), bf16),
            pltpu.VMEM((depth, 4, CHUNKS, rows, chunk), bf16),
            pltpu.VMEM((depth + 1, 4, rows, PAD), f32),
            pltpu.VMEM((slots, nt, share * FINE, COARSE * rows), bf16),
            pltpu.VMEM((slots, nt, share * FINE, COARSE * rows), bf16),
            dma,
            dma((nt,)), dma((nt,)),
            dma((2,)), dma((2,)),
            dma((CHUNKS,)), dma((CHUNKS,)),
            dma((depth, 4, CHUNKS)), dma((depth, 4, CHUNKS)),
            dma((depth + 1, 3)), dma((depth + 1, 3)),
            dma((slots, nt)), dma((slots, nt)),
        ],
        compiler_params=pltpu.CompilerParams(collective_id=0, has_side_effects=True),
    )(traces, partners, lengths)
    found = found.reshape(share, slots, rows, LAGS)
    return jnp.transpose(found, (0, 3, 1, 2))


def solution(mesh):
    placed = (P("block", "tm"), P(), P())
    return jax.shard_map(
        functools.partial(shards, mesh.shape["block"], mesh.shape["tm"]),
        mesh=mesh,
        in_specs=placed,
        out_specs=P(("block", "tm"), None, None, None),
        check_vma=False,
    )
```

```python
import functools

import jax
import jax.numpy as jnp
from jax import lax
from jax.experimental import pallas as pl
from jax.experimental.pallas import tpu as pltpu
from jax.sharding import PartitionSpec as P

HALF = 50
ROUNDS = 2
LAGS = 101
FINE = 8
COARSE = 13
PAD = 128
CHUNKS = 8
MESH = pl.DeviceIdType.MESH


def kernel(
    nb, nt, rows, width,
    traces_ref, partners_ref, lengths_ref, out_ref,
    raw, edge, esend, erecv, ext, lhs, rhs, padded, cross, hops, norms, part, parts,
    load_sem, esend_sem, erecv_sem, hsend_sem, hrecv_sem,
    csend_sem, crecv_sem, bsend_sem, brecv_sem,
    nsend_sem, nrecv_sem, psend_sem, precv_sem,
):
    b = lax.axis_index("block")
    t = lax.axis_index("tm")
    bits = nb.bit_length() - 2
    half_mask = nb // 2
    share = rows // nt
    chunk = width // CHUNKS
    span = width + PAD
    f32, bf16 = jnp.float32, jnp.bfloat16

    def at_tm(i):
        return (b, lax.rem(t + i, nt))

    def flip(mask):
        size = 2 * mask
        low = lax.rem(b, size)
        return (b - low + lax.rem(low + mask, size), t)

    barrier = pltpu.get_barrier_semaphore()
    load = pltpu.make_async_copy(traces_ref, raw, load_sem)
    load.start()
    peers = [at_tm(i) for i in range(1, nt)] + [flip(1 << i) for i in range(bits + 1)]
    for peer in peers:
        pl.semaphore_signal(barrier, inc=1, device_id=peer, device_id_type=MESH)

    def gap(values, index, first):
        length = lengths_ref[index]
        begin = length // 2
        position = first + lax.broadcasted_iota(jnp.int32, values.shape, 1)
        recorded = (position < begin) | (position >= begin + width - length)
        return jnp.where(recorded, values, 0.0)

    load.wait()
    total = jnp.zeros((rows, PAD), f32)
    for ch in range(CHUNKS):
        piece = gap(raw[:, ch * chunk : (ch + 1) * chunk], t, ch * chunk)
        cross[0, ch] = piece.astype(bf16)
        for i in range(chunk // PAD):
            tile = piece[:, i * PAD : (i + 1) * PAD]
            total = total + tile * tile
    esend[...] = total
    pl.semaphore_wait(barrier, len(peers))

    energy = []
    for i in range(1, nt):
        copy = pltpu.make_async_remote_copy(
            esend, erecv.at[i], esend_sem.at[i], erecv_sem.at[i],
            device_id=at_tm(i), device_id_type=MESH,
        )
        copy.start()
        energy.append(copy)
    to_next = pltpu.make_async_remote_copy(
        raw.at[:, pl.ds(width - PAD, PAD)], edge.at[0], hsend_sem.at[0], hrecv_sem.at[0],
        device_id=at_tm(1), device_id_type=MESH,
    )
    to_previous = pltpu.make_async_remote_copy(
        raw.at[:, pl.ds(0, PAD)], edge.at[1], hsend_sem.at[1], hrecv_sem.at[1],
        device_id=at_tm(nt - 1), device_id_type=MESH,
    )
    to_next.start()
    to_previous.start()
    crossing = []
    for ch in range(CHUNKS):
        copy = pltpu.make_async_remote_copy(
            cross.at[0, ch], cross.at[1, ch], csend_sem.at[ch], crecv_sem.at[ch],
            device_id=flip(half_mask), device_id_type=MESH,
        )
        copy.start()
        crossing.append(copy)

    summed = lengths_ref[0]
    for i in range(1, nt):
        summed = summed + lengths_ref[i]
    count = jnp.full((1, 1), summed, jnp.int32).astype(f32)
    padded[:, :PAD] = jnp.zeros((rows, PAD), bf16)
    padded[:, PAD + width :] = jnp.zeros((rows, PAD), bf16)

    for copy in energy:
        copy.wait_recv()
    for i in range(1, nt):
        total = total + erecv[i]
    power = jnp.sum(total, axis=1, keepdims=True) / count + 1e-06
    root = jnp.sqrt(power)

    def whiten(values):
        return (values / root).astype(bf16)

    norms[0, 0] = jnp.broadcast_to(1.0 / root, (rows, PAD))

    def pass_norm(stage, mask):
        copy = pltpu.make_async_remote_copy(
            norms.at[stage, 0], norms.at[stage, 1], nsend_sem.at[stage], nrecv_sem.at[stage],
            device_id=flip(mask), device_id_type=MESH,
        )
        copy.start()
        return copy

    normed = [pass_norm(0, half_mask)]
    for ch in range(CHUNKS):
        piece = whiten(gap(raw[:, ch * chunk : (ch + 1) * chunk], t, ch * chunk))
        ext[:, PAD + ch * chunk : PAD + (ch + 1) * chunk] = piece.astype(f32)
        padded[:, PAD + ch * chunk : PAD + (ch + 1) * chunk] = piece

    to_next.wait_recv()
    to_previous.wait_recv()
    before = whiten(gap(edge[0], lax.rem(t + nt - 1, nt), width - PAD)).astype(f32)
    after = whiten(gap(edge[1], lax.rem(t + 1, nt), 0)).astype(f32)
    ext[:, :PAD] = jnp.where(t > 0, before, 0.0)
    ext[:, PAD + width :] = jnp.where(t < nt - 1, after, 0.0)

    top = FINE * (COARSE - 1) - HALF
    for pair in range(rows // 2):
        both = []
        for c in (2 * pair, 2 * pair + 1):
            row = jnp.broadcast_to(ext[c : c + 1, :], (FINE, width + 2 * PAD))
            rolled = pltpu.roll(
                row, width + 2 * PAD - (PAD - top), 1, stride=1, stride_axis=0
            )
            both.append(rolled[:, :span])
        lhs[2 * FINE * pair : 2 * FINE * (pair + 1), :] = jnp.concatenate(both, axis=0).astype(bf16)

    sends = []

    def correlate(slot):
        for a in range(COARSE):
            offset = PAD - FINE * (COARSE - 1) + FINE * a
            rhs[a * rows : (a + 1) * rows, :] = padded[:, offset : offset + span]
        product = lax.dot_general(
            lhs[...], rhs[...], (((1,), (1,)), ((), ())), preferred_element_type=f32
        )
        part[slot] = product.astype(bf16).reshape(nt, share * FINE, COARSE * rows)
        for i in range(1, nt):
            copy = pltpu.make_async_remote_copy(
                part.at[slot, lax.rem(t + i, nt)], parts.at[slot, i],
                psend_sem.at[slot, i], precv_sem.at[slot, i],
                device_id=at_tm(i), device_id_type=MESH,
            )
            copy.start()
            sends.append(copy)

    correlate(0)

    first_mask = partners_ref[0, 0]
    second_mask = partners_ref[1, 0]
    swapped = first_mask != half_mask
    other = jnp.where(swapped, first_mask, second_mask)
    crossed = other >= half_mask

    stages = [[] for _ in range(bits)]

    def forward(stage, ch, piece):
        hops[stage, 0, ch] = piece
        copy = pltpu.make_async_remote_copy(
            hops.at[stage, 0, ch], hops.at[stage, 1, ch],
            bsend_sem.at[stage, ch], brecv_sem.at[stage, ch],
            device_id=flip(1 << stage), device_id_type=MESH,
        )
        copy.start()
        stages[stage].append(copy)

    def place(ch, piece):
        padded[:, PAD + ch * chunk : PAD + (ch + 1) * chunk] = piece

    for ch in range(CHUNKS):
        crossing[ch].wait_recv()
        arrived = cross[1, ch]
        forward(0, ch, jnp.where(crossed, arrived, cross[0, ch]))
        place(ch, arrived)
    normed[0].wait_recv()
    norms[1, 0] = jnp.where(crossed, norms[0, 1], norms[0, 0])
    normed.append(pass_norm(1, 1))
    correlate(1)
    for stage in range(bits):
        taken = lax.rem(other // (1 << stage), 2) == 1
        for ch in range(CHUNKS):
            stages[stage][ch].wait_recv()
            piece = jnp.where(taken, hops[stage, 1, ch], hops[stage, 0, ch])
            if stage < bits - 1:
                forward(stage + 1, ch, piece)
            else:
                place(ch, piece)
        normed[stage + 1].wait_recv()
        factor = jnp.where(taken, norms[stage + 1, 1], norms[stage + 1, 0])
        if stage < bits - 1:
            norms[stage + 2, 0] = factor
            normed.append(pass_norm(stage + 2, 2 << stage))
    correlate(2)

    scale = 1.0 / jnp.sqrt(count)
    results = []
    for slot in range(ROUNDS + 1):
        mine = part[slot, t].astype(f32)
        for i in range(1, nt):
            sends[slot * (nt - 1) + i - 1].wait_recv()
            mine = mine + parts[slot, i].astype(f32)
        results.append(mine * scale)
    ordered = [
        results[0],
        jnp.where(swapped, results[2], results[1]),
        jnp.where(swapped, results[1], results[2]),
    ]
    near = norms[0, 1]
    factors = jnp.concatenate(
        [
            jnp.ones((rows, PAD), f32),
            jnp.where(swapped, factor, near),
            jnp.where(swapped, near, factor),
        ],
        axis=0,
    )
    fine = lax.broadcasted_iota(jnp.int32, (FINE, rows), 0)
    column = lax.broadcasted_iota(jnp.int32, (FINE, rows), 1)
    for c in range(share):
        lags = []
        for a in range(COARSE):
            tiles = [
                x[c * FINE : (c + 1) * FINE, a * rows : (a + 1) * rows] for x in ordered
            ]
            if a == HALF // FINE:
                killed = (fine == HALF % FINE) & (column == t * share + c)
                tiles[0] = jnp.where(killed, 0.0, tiles[0])
            spare = PAD - len(tiles) * rows
            lags.append(jnp.concatenate(tiles + [jnp.zeros((FINE, spare), f32)], axis=1))
        lags.append(jnp.zeros((PAD - FINE * COARSE, PAD), f32))
        turned = jnp.concatenate(lags, axis=0).T
        out_ref[c] = (turned[: len(ordered) * rows] * factors)[:, :LAGS]

    for copy in energy + [to_next, to_previous] + crossing + sum(stages, []) + normed + sends:
        copy.wait_send()


def shards(nb, nt, traces, partners, lengths):
    rows, width = traces.shape
    share = rows // nt
    bits = nb.bit_length() - 2
    chunk = width // CHUNKS
    span = width + PAD
    f32, bf16 = jnp.float32, jnp.bfloat16
    dma = pltpu.SemaphoreType.DMA
    slots = ROUNDS + 1
    found = pl.pallas_call(
        functools.partial(kernel, nb, nt, rows, width),
        out_shape=pltpu.VMEM((share, slots * rows, LAGS), f32),
        in_specs=[
            pl.BlockSpec(memory_space=pl.ANY),
            pl.BlockSpec(memory_space=pltpu.SMEM),
            pl.BlockSpec(memory_space=pltpu.SMEM),
        ],
        out_specs=pl.BlockSpec(memory_space=pltpu.VMEM),
        scratch_shapes=[
            pltpu.VMEM((rows, width), f32),
            pltpu.VMEM((2, rows, PAD), f32),
            pltpu.VMEM((rows, PAD), f32),
            pltpu.VMEM((nt, rows, PAD), f32),
            pltpu.VMEM((rows, width + 2 * PAD), f32),
            pltpu.VMEM((rows * FINE, span), bf16),
            pltpu.VMEM((COARSE * rows, span), bf16),
            pltpu.VMEM((rows, width + 2 * PAD), bf16),
            pltpu.VMEM((2, CHUNKS, rows, chunk), bf16),
            pltpu.VMEM((bits, 2, CHUNKS, rows, chunk), bf16),
            pltpu.VMEM((bits + 1, 2, rows, PAD), f32),
            pltpu.VMEM((slots, nt, share * FINE, COARSE * rows), bf16),
            pltpu.VMEM((slots, nt, share * FINE, COARSE * rows), bf16),
            dma,
            dma((nt,)), dma((nt,)),
            dma((2,)), dma((2,)),
            dma((CHUNKS,)), dma((CHUNKS,)),
            dma((bits, CHUNKS)), dma((bits, CHUNKS)),
            dma((bits + 1,)), dma((bits + 1,)),
            dma((slots, nt)), dma((slots, nt)),
        ],
        compiler_params=pltpu.CompilerParams(collective_id=0, has_side_effects=True),
    )(traces, partners, lengths)
    found = found.reshape(share, slots, rows, LAGS)
    return jnp.transpose(found, (0, 3, 1, 2))


def solution(mesh):
    placed = (P("block", "tm"), P(), P())
    return jax.shard_map(
        functools.partial(shards, mesh.shape["block"], mesh.shape["tm"]),
        mesh=mesh,
        in_specs=placed,
        out_specs=P(("block", "tm"), None, None, None),
        check_vma=False,
    )
```

```python
import functools

import jax
import jax.numpy as jnp
from jax import lax
from jax.experimental import pallas as pl
from jax.experimental.pallas import tpu as pltpu
from jax.sharding import PartitionSpec as P

HALF = 50
ROUNDS = 2
LAGS = 101
FINE = 8
COARSE = 13
PAD = 128
CHUNKS = 8
MESH = pl.DeviceIdType.MESH


def kernel(
    nb, nt, rows, width,
    traces_ref, partners_ref, lengths_ref, out_ref,
    raw, edge, esend, erecv, ext, lhs, rhs, padded, cross, hops, norms, part, parts,
    load_sem, esend_sem, erecv_sem, hsend_sem, hrecv_sem,
    csend_sem, crecv_sem, bsend_sem, brecv_sem,
    nsend_sem, nrecv_sem, psend_sem, precv_sem,
):
    b = lax.axis_index("block")
    t = lax.axis_index("tm")
    bits = nb.bit_length() - 2
    half_mask = nb // 2
    share = rows // nt
    chunk = width // CHUNKS
    span = width + PAD
    f32, bf16 = jnp.float32, jnp.bfloat16

    def at_tm(i):
        return (b, lax.rem(t + i, nt))

    def flip(mask):
        size = 2 * mask
        low = lax.rem(b, size)
        return (b - low + lax.rem(low + mask, size), t)

    barrier = pltpu.get_barrier_semaphore()
    load = pltpu.make_async_copy(traces_ref, raw, load_sem)
    load.start()
    peers = [at_tm(i) for i in range(1, nt)] + [flip(1 << i) for i in range(bits + 1)]
    for peer in peers:
        pl.semaphore_signal(barrier, inc=1, device_id=peer, device_id_type=MESH)

    def gap(values, index, first):
        length = lengths_ref[index]
        begin = length // 2
        position = first + lax.broadcasted_iota(jnp.int32, values.shape, 1)
        recorded = (position < begin) | (position >= begin + width - length)
        return jnp.where(recorded, values, 0.0)

    load.wait()
    total = jnp.zeros((rows, PAD), f32)
    for ch in range(CHUNKS):
        piece = gap(raw[:, ch * chunk : (ch + 1) * chunk], t, ch * chunk)
        cross[0, ch] = piece.astype(bf16)
        for i in range(chunk // PAD):
            tile = piece[:, i * PAD : (i + 1) * PAD]
            total = total + tile * tile
    esend[...] = total
    pl.semaphore_wait(barrier, len(peers))

    energy = []
    for i in range(1, nt):
        copy = pltpu.make_async_remote_copy(
            esend, erecv.at[i], esend_sem.at[i], erecv_sem.at[i],
            device_id=at_tm(i), device_id_type=MESH,
        )
        copy.start()
        energy.append(copy)
    to_next = pltpu.make_async_remote_copy(
        raw.at[:, pl.ds(width - PAD, PAD)], edge.at[0], hsend_sem.at[0], hrecv_sem.at[0],
        device_id=at_tm(1), device_id_type=MESH,
    )
    to_previous = pltpu.make_async_remote_copy(
        raw.at[:, pl.ds(0, PAD)], edge.at[1], hsend_sem.at[1], hrecv_sem.at[1],
        device_id=at_tm(nt - 1), device_id_type=MESH,
    )
    to_next.start()
    to_previous.start()
    crossing = []
    for ch in range(CHUNKS):
        copy = pltpu.make_async_remote_copy(
            cross.at[0, ch], cross.at[1, ch], csend_sem.at[ch], crecv_sem.at[ch],
            device_id=flip(half_mask), device_id_type=MESH,
        )
        copy.start()
        crossing.append(copy)

    summed = lengths_ref[0]
    for i in range(1, nt):
        summed = summed + lengths_ref[i]
    count = jnp.full((1, 1), summed, jnp.int32).astype(f32)
    padded[:, :PAD] = jnp.zeros((rows, PAD), bf16)
    padded[:, PAD + width :] = jnp.zeros((rows, PAD), bf16)

    for copy in energy:
        copy.wait_recv()
    for i in range(1, nt):
        total = total + erecv[i]
    power = jnp.sum(total, axis=1, keepdims=True) / count + 1e-06
    root = jnp.sqrt(power)

    def whiten(values):
        return (values / root).astype(bf16)

    norms[0, 0] = jnp.broadcast_to(1.0 / root, (rows, PAD))

    def pass_norm(stage, mask):
        copy = pltpu.make_async_remote_copy(
            norms.at[stage, 0], norms.at[stage, 1], nsend_sem.at[stage], nrecv_sem.at[stage],
            device_id=flip(mask), device_id_type=MESH,
        )
        copy.start()
        return copy

    normed = [pass_norm(0, half_mask)]
    for ch in range(CHUNKS):
        piece = whiten(gap(raw[:, ch * chunk : (ch + 1) * chunk], t, ch * chunk))
        ext[:, PAD + ch * chunk : PAD + (ch + 1) * chunk] = piece.astype(f32)
        padded[:, PAD + ch * chunk : PAD + (ch + 1) * chunk] = piece

    to_next.wait_recv()
    to_previous.wait_recv()
    before = whiten(gap(edge[0], lax.rem(t + nt - 1, nt), width - PAD)).astype(f32)
    after = whiten(gap(edge[1], lax.rem(t + 1, nt), 0)).astype(f32)
    ext[:, :PAD] = jnp.where(t > 0, before, 0.0)
    ext[:, PAD + width :] = jnp.where(t < nt - 1, after, 0.0)

    top = FINE * (COARSE - 1) - HALF
    for pair in range(rows // 2):
        both = []
        for c in (2 * pair, 2 * pair + 1):
            row = jnp.broadcast_to(ext[c : c + 1, :], (FINE, width + 2 * PAD))
            rolled = pltpu.roll(
                row, width + 2 * PAD - (PAD - top), 1, stride=1, stride_axis=0
            )
            both.append(rolled[:, :span])
        lhs[2 * FINE * pair : 2 * FINE * (pair + 1), :] = jnp.concatenate(both, axis=0).astype(bf16)

    sends = []

    def correlate(slot):
        for a in range(COARSE):
            offset = PAD - FINE * (COARSE - 1) + FINE * a
            rhs[a * rows : (a + 1) * rows, :] = padded[:, offset : offset + span]
        product = lax.dot_general(
            lhs[...], rhs[...], (((1,), (1,)), ((), ())), preferred_element_type=f32
        )
        part[slot] = product.astype(bf16).reshape(nt, share * FINE, COARSE * rows)
        for i in range(1, nt):
            copy = pltpu.make_async_remote_copy(
                part.at[slot, lax.rem(t + i, nt)], parts.at[slot, i],
                psend_sem.at[slot, i], precv_sem.at[slot, i],
                device_id=at_tm(i), device_id_type=MESH,
            )
            copy.start()
            sends.append(copy)

    correlate(0)

    first_mask = partners_ref[0, 0]
    second_mask = partners_ref[1, 0]
    swapped = first_mask != half_mask
    other = jnp.where(swapped, first_mask, second_mask)
    crossed = other >= half_mask

    stages = [[] for _ in range(bits)]

    def forward(stage, ch, piece):
        hops[stage, 0, ch] = piece
        copy = pltpu.make_async_remote_copy(
            hops.at[stage, 0, ch], hops.at[stage, 1, ch],
            bsend_sem.at[stage, ch], brecv_sem.at[stage, ch],
            device_id=flip(1 << stage), device_id_type=MESH,
        )
        copy.start()
        stages[stage].append(copy)

    def place(ch, piece):
        padded[:, PAD + ch * chunk : PAD + (ch + 1) * chunk] = piece

    for ch in range(CHUNKS):
        crossing[ch].wait_recv()
        arrived = cross[1, ch]
        forward(0, ch, jnp.where(crossed, arrived, cross[0, ch]))
        place(ch, arrived)
    normed[0].wait_recv()
    norms[1, 0] = jnp.where(crossed, norms[0, 1], norms[0, 0])
    normed.append(pass_norm(1, 1))
    correlate(1)
    for stage in range(bits):
        taken = lax.rem(other // (1 << stage), 2) == 1
        for ch in range(CHUNKS):
            stages[stage][ch].wait_recv()
            piece = jnp.where(taken, hops[stage, 1, ch], hops[stage, 0, ch])
            if stage < bits - 1:
                forward(stage + 1, ch, piece)
            else:
                place(ch, piece)
        if stage < bits - 1:
            normed[stage + 1].wait_recv()
            norms[stage + 2, 0] = jnp.where(taken, norms[stage + 1, 1], norms[stage + 1, 0])
            normed.append(pass_norm(stage + 2, 2 << stage))
    correlate(2)

    scale = 1.0 / jnp.sqrt(count)
    results = []
    for slot in range(ROUNDS + 1):
        mine = part[slot, t].astype(f32)
        for i in range(1, nt):
            sends[slot * (nt - 1) + i - 1].wait_recv()
            mine = mine + parts[slot, i].astype(f32)
        results.append(mine * scale)
    ordered = [
        results[0],
        jnp.where(swapped, results[2], results[1]),
        jnp.where(swapped, results[1], results[2]),
    ]
    near = norms[0, 1]
    normed[bits].wait_recv()
    factor = jnp.where(taken, norms[bits, 1], norms[bits, 0])
    factors = jnp.concatenate(
        [
            jnp.ones((rows, PAD), f32),
            jnp.where(swapped, factor, near),
            jnp.where(swapped, near, factor),
        ],
        axis=0,
    )
    fine = lax.broadcasted_iota(jnp.int32, (FINE, rows), 0)
    column = lax.broadcasted_iota(jnp.int32, (FINE, rows), 1)
    for c in range(share):
        lags = []
        for a in range(COARSE):
            tiles = [
                x[c * FINE : (c + 1) * FINE, a * rows : (a + 1) * rows] for x in ordered
            ]
            if a == HALF // FINE:
                killed = (fine == HALF % FINE) & (column == t * share + c)
                tiles[0] = jnp.where(killed, 0.0, tiles[0])
            spare = PAD - len(tiles) * rows
            lags.append(jnp.concatenate(tiles + [jnp.zeros((FINE, spare), f32)], axis=1))
        lags.append(jnp.zeros((PAD - FINE * COARSE, PAD), f32))
        turned = jnp.concatenate(lags, axis=0).T
        out_ref[c] = (turned[: len(ordered) * rows] * factors)[:, :LAGS]

    for copy in energy + [to_next, to_previous] + crossing + sum(stages, []) + normed + sends:
        copy.wait_send()


def shards(nb, nt, traces, partners, lengths):
    rows, width = traces.shape
    share = rows // nt
    bits = nb.bit_length() - 2
    chunk = width // CHUNKS
    span = width + PAD
    f32, bf16 = jnp.float32, jnp.bfloat16
    dma = pltpu.SemaphoreType.DMA
    slots = ROUNDS + 1
    found = pl.pallas_call(
        functools.partial(kernel, nb, nt, rows, width),
        out_shape=pltpu.VMEM((share, slots * rows, LAGS), f32),
        in_specs=[
            pl.BlockSpec(memory_space=pl.ANY),
            pl.BlockSpec(memory_space=pltpu.SMEM),
            pl.BlockSpec(memory_space=pltpu.SMEM),
        ],
        out_specs=pl.BlockSpec(memory_space=pltpu.VMEM),
        scratch_shapes=[
            pltpu.VMEM((rows, width), f32),
            pltpu.VMEM((2, rows, PAD), f32),
            pltpu.VMEM((rows, PAD), f32),
            pltpu.VMEM((nt, rows, PAD), f32),
            pltpu.VMEM((rows, width + 2 * PAD), f32),
            pltpu.VMEM((rows * FINE, span), bf16),
            pltpu.VMEM((COARSE * rows, span), bf16),
            pltpu.VMEM((rows, width + 2 * PAD), bf16),
            pltpu.VMEM((2, CHUNKS, rows, chunk), bf16),
            pltpu.VMEM((bits, 2, CHUNKS, rows, chunk), bf16),
            pltpu.VMEM((bits + 1, 2, rows, PAD), f32),
            pltpu.VMEM((slots, nt, share * FINE, COARSE * rows), bf16),
            pltpu.VMEM((slots, nt, share * FINE, COARSE * rows), bf16),
            dma,
            dma((nt,)), dma((nt,)),
            dma((2,)), dma((2,)),
            dma((CHUNKS,)), dma((CHUNKS,)),
            dma((bits, CHUNKS)), dma((bits, CHUNKS)),
            dma((bits + 1,)), dma((bits + 1,)),
            dma((slots, nt)), dma((slots, nt)),
        ],
        compiler_params=pltpu.CompilerParams(collective_id=0, has_side_effects=True),
    )(traces, partners, lengths)
    found = found.reshape(share, slots, rows, LAGS)
    return jnp.transpose(found, (0, 3, 1, 2))


def solution(mesh):
    placed = (P("block", "tm"), P(), P())
    return jax.shard_map(
        functools.partial(shards, mesh.shape["block"], mesh.shape["tm"]),
        mesh=mesh,
        in_specs=placed,
        out_specs=P(("block", "tm"), None, None, None),
        check_vma=False,
    )
```

```python
import functools

import jax
import jax.numpy as jnp
from jax import lax
from jax.experimental import pallas as pl
from jax.experimental.pallas import tpu as pltpu
from jax.sharding import PartitionSpec as P

HALF = 50
ROUNDS = 2
LAGS = 101
FINE = 8
COARSE = 13
PAD = 128
CHUNKS = 8
MESH = pl.DeviceIdType.MESH


def kernel(
    nb, nt, rows, width,
    traces_ref, partners_ref, lengths_ref, out_ref,
    raw, edge, esend, erecv, ext, lhs, rhs, padded, cross, hops, norms, part, parts,
    load_sem, esend_sem, erecv_sem, hsend_sem, hrecv_sem,
    csend_sem, crecv_sem, bsend_sem, brecv_sem,
    nsend_sem, nrecv_sem, psend_sem, precv_sem,
):
    b = lax.axis_index("block")
    t = lax.axis_index("tm")
    bits = nb.bit_length() - 2
    half_mask = nb // 2
    share = rows // nt
    chunk = width // CHUNKS
    span = width + PAD
    f32, bf16 = jnp.float32, jnp.bfloat16

    def at_tm(i):
        return (b, lax.rem(t + i, nt))

    def flip(mask):
        size = 2 * mask
        low = lax.rem(b, size)
        return (b - low + lax.rem(low + mask, size), t)

    barrier = pltpu.get_barrier_semaphore()
    load = pltpu.make_async_copy(traces_ref, raw, load_sem)
    load.start()
    peers = [at_tm(i) for i in range(1, nt)] + [flip(1 << i) for i in range(bits + 1)]
    for peer in peers:
        pl.semaphore_signal(barrier, inc=1, device_id=peer, device_id_type=MESH)

    def gap(values, index, first):
        length = lengths_ref[index]
        begin = length // 2
        position = first + lax.broadcasted_iota(jnp.int32, values.shape, 1)
        recorded = (position < begin) | (position >= begin + width - length)
        return jnp.where(recorded, values, 0.0)

    load.wait()
    total = jnp.zeros((rows, PAD), f32)
    for ch in range(CHUNKS):
        piece = gap(raw[:, ch * chunk : (ch + 1) * chunk], t, ch * chunk)
        cross[0, ch] = piece.astype(bf16)
        for i in range(chunk // PAD):
            tile = piece[:, i * PAD : (i + 1) * PAD]
            total = total + tile * tile
    esend[...] = total
    pl.semaphore_wait(barrier, len(peers))

    energy = []
    for i in range(1, nt):
        copy = pltpu.make_async_remote_copy(
            esend, erecv.at[i], esend_sem.at[i], erecv_sem.at[i],
            device_id=at_tm(i), device_id_type=MESH,
        )
        copy.start()
        energy.append(copy)
    to_next = pltpu.make_async_remote_copy(
        raw.at[:, pl.ds(width - PAD, PAD)], edge.at[0], hsend_sem.at[0], hrecv_sem.at[0],
        device_id=at_tm(1), device_id_type=MESH,
    )
    to_previous = pltpu.make_async_remote_copy(
        raw.at[:, pl.ds(0, PAD)], edge.at[1], hsend_sem.at[1], hrecv_sem.at[1],
        device_id=at_tm(nt - 1), device_id_type=MESH,
    )
    to_next.start()
    to_previous.start()
    crossing = []
    for ch in range(CHUNKS):
        copy = pltpu.make_async_remote_copy(
            cross.at[0, ch], cross.at[1, ch], csend_sem.at[ch], crecv_sem.at[ch],
            device_id=flip(half_mask), device_id_type=MESH,
        )
        copy.start()
        crossing.append(copy)

    summed = lengths_ref[0]
    for i in range(1, nt):
        summed = summed + lengths_ref[i]
    count = jnp.full((1, 1), summed, jnp.int32).astype(f32)
    padded[:, :PAD] = jnp.zeros((rows, PAD), bf16)
    padded[:, PAD + width :] = jnp.zeros((rows, PAD), bf16)

    for copy in energy:
        copy.wait_recv()
    for i in range(1, nt):
        total = total + erecv[i]
    power = jnp.sum(total, axis=1, keepdims=True) / count + 1e-06
    root = jnp.sqrt(power)

    def whiten(values):
        return (values / root).astype(bf16)

    norms[0, 0] = jnp.broadcast_to(1.0 / root, (rows, PAD))

    def pass_norm(stage, mask):
        copy = pltpu.make_async_remote_copy(
            norms.at[stage, 0], norms.at[stage, 1], nsend_sem.at[stage], nrecv_sem.at[stage],
            device_id=flip(mask), device_id_type=MESH,
        )
        copy.start()
        return copy

    normed = [pass_norm(0, half_mask)]
    for ch in range(CHUNKS):
        piece = whiten(gap(raw[:, ch * chunk : (ch + 1) * chunk], t, ch * chunk))
        ext[:, PAD + ch * chunk : PAD + (ch + 1) * chunk] = piece.astype(f32)
        padded[:, PAD + ch * chunk : PAD + (ch + 1) * chunk] = piece

    to_next.wait_recv()
    to_previous.wait_recv()
    before = whiten(gap(edge[0], lax.rem(t + nt - 1, nt), width - PAD)).astype(f32)
    after = whiten(gap(edge[1], lax.rem(t + 1, nt), 0)).astype(f32)
    ext[:, :PAD] = jnp.where(t > 0, before, 0.0)
    ext[:, PAD + width :] = jnp.where(t < nt - 1, after, 0.0)

    top = FINE * (COARSE - 1) - HALF
    for pair in range(rows // 2):
        both = []
        for c in (2 * pair, 2 * pair + 1):
            row = jnp.broadcast_to(ext[c : c + 1, :], (FINE, width + 2 * PAD))
            rolled = pltpu.roll(
                row, width + 2 * PAD - (PAD - top), 1, stride=1, stride_axis=0
            )
            both.append(rolled[:, :span])
        lhs[2 * FINE * pair : 2 * FINE * (pair + 1), :] = jnp.concatenate(both, axis=0).astype(bf16)

    sends = []

    def correlate(slot):
        for a in range(COARSE):
            offset = PAD - FINE * (COARSE - 1) + FINE * a
            rhs[a * rows : (a + 1) * rows, :] = padded[:, offset : offset + span]
        product = lax.dot_general(
            lhs[...], rhs[...], (((1,), (1,)), ((), ())), preferred_element_type=f32
        )
        part[slot] = product.astype(bf16).reshape(nt, share * FINE, COARSE * rows)
        for i in range(1, nt):
            copy = pltpu.make_async_remote_copy(
                part.at[slot, lax.rem(t + i, nt)], parts.at[slot, i],
                psend_sem.at[slot, i], precv_sem.at[slot, i],
                device_id=at_tm(i), device_id_type=MESH,
            )
            copy.start()
            sends.append(copy)

    correlate(0)

    first_mask = partners_ref[0, 0]
    second_mask = partners_ref[1, 0]
    swapped = first_mask != half_mask
    other = jnp.where(swapped, first_mask, second_mask)
    crossed = other >= half_mask

    stages = [[] for _ in range(bits)]

    def forward(stage, ch, piece):
        hops[stage, 0, ch] = piece
        copy = pltpu.make_async_remote_copy(
            hops.at[stage, 0, ch], hops.at[stage, 1, ch],
            bsend_sem.at[stage, ch], brecv_sem.at[stage, ch],
            device_id=flip(1 << stage), device_id_type=MESH,
        )
        copy.start()
        stages[stage].append(copy)

    def place(ch, piece):
        padded[:, PAD + ch * chunk : PAD + (ch + 1) * chunk] = piece

    for ch in range(CHUNKS):
        crossing[ch].wait_recv()
        arrived = cross[1, ch]
        forward(0, ch, jnp.where(crossed, arrived, cross[0, ch]))
        place(ch, arrived)
    normed[0].wait_recv()
    norms[1, 0] = jnp.where(crossed, norms[0, 1], norms[0, 0])
    normed.append(pass_norm(1, 1))
    correlate(1)
    for stage in range(bits):
        taken = lax.rem(other // (1 << stage), 2) == 1
        for ch in range(CHUNKS):
            stages[stage][ch].wait_recv()
            piece = jnp.where(taken, hops[stage, 1, ch], hops[stage, 0, ch])
            if stage < bits - 1:
                forward(stage + 1, ch, piece)
            else:
                place(ch, piece)
        if stage < bits - 1:
            normed[stage + 1].wait_recv()
            norms[stage + 2, 0] = jnp.where(taken, norms[stage + 1, 1], norms[stage + 1, 0])
            normed.append(pass_norm(stage + 2, 2 << stage))
    correlate(2)

    scale = 1.0 / jnp.sqrt(count)
    full = COARSE * rows // PAD
    quad = PAD // rows
    lane = lax.broadcasted_iota(jnp.int32, (full * FINE, PAD), 1)

    def gathered(slot):
        mine = part[slot, t].astype(f32)
        for i in range(1, nt):
            sends[slot * (nt - 1) + i - 1].wait_recv()
            mine = mine + parts[slot, i].astype(f32)
        mine = mine * scale
        out = []
        for c0 in range(0, share, quad):
            blocks = []
            rests = []
            for c in range(c0, min(c0 + quad, share)):
                own = mine[c * FINE : (c + 1) * FINE]
                blocks.append(jnp.concatenate(
                    [own[:, j * PAD : (j + 1) * PAD] for j in range(full)], axis=0
                ))
                rests.append(own[:, full * PAD :])
            real = len(blocks)
            blocks += [jnp.zeros((full * FINE, PAD), f32)] * (quad - real)
            step = 1
            while step < quad:
                odd = lax.rem(lane // (rows * step), 2) == 1
                for i in range(quad):
                    if not i & step:
                        one, two = blocks[i], blocks[i + step]
                        blocks[i] = jnp.where(odd, pltpu.roll(two, rows * step, 1), one)
                        blocks[i + step] = jnp.where(odd, two, pltpu.roll(one, PAD - rows * step, 1))
                step *= 2
            lags = [
                blocks[i][j * FINE : (j + 1) * FINE] for j in range(full) for i in range(quad)
            ]
            if real < quad:
                rests.append(jnp.zeros((FINE, PAD - real * rows), f32))
            lags.append(jnp.concatenate(rests, axis=1))
            lags.append(jnp.zeros((PAD - FINE * COARSE, PAD), f32))
            turned = jnp.concatenate(lags, axis=0).T
            out.append(turned.reshape(quad, rows, PAD)[:real])
        return jnp.concatenate(out, axis=0)

    shape = (share, rows, PAD)
    index, column, lag = (lax.broadcasted_iota(jnp.int32, shape, i) for i in range(3))
    killed = (lag == HALF) & (column == t * share + index)
    out_ref[:, :rows, :] = jnp.where(killed, 0.0, gathered(0))[:, :, :LAGS]
    near = gathered(1) * norms[0, 1][None]
    normed[bits].wait_recv()
    factor = jnp.where(taken, norms[bits, 1], norms[bits, 0])
    far = gathered(2) * factor[None]
    out_ref[:, rows : 2 * rows, :] = jnp.where(swapped, far, near)[:, :, :LAGS]
    out_ref[:, 2 * rows :, :] = jnp.where(swapped, near, far)[:, :, :LAGS]

    for copy in energy + [to_next, to_previous] + crossing + sum(stages, []) + normed + sends:
        copy.wait_send()


def shards(nb, nt, traces, partners, lengths):
    rows, width = traces.shape
    share = rows // nt
    bits = nb.bit_length() - 2
    chunk = width // CHUNKS
    span = width + PAD
    f32, bf16 = jnp.float32, jnp.bfloat16
    dma = pltpu.SemaphoreType.DMA
    slots = ROUNDS + 1
    found = pl.pallas_call(
        functools.partial(kernel, nb, nt, rows, width),
        out_shape=pltpu.VMEM((share, slots * rows, LAGS), f32),
        in_specs=[
            pl.BlockSpec(memory_space=pl.ANY),
            pl.BlockSpec(memory_space=pltpu.SMEM),
            pl.BlockSpec(memory_space=pltpu.SMEM),
        ],
        out_specs=pl.BlockSpec(memory_space=pltpu.VMEM),
        scratch_shapes=[
            pltpu.VMEM((rows, width), f32),
            pltpu.VMEM((2, rows, PAD), f32),
            pltpu.VMEM((rows, PAD), f32),
            pltpu.VMEM((nt, rows, PAD), f32),
            pltpu.VMEM((rows, width + 2 * PAD), f32),
            pltpu.VMEM((rows * FINE, span), bf16),
            pltpu.VMEM((COARSE * rows, span), bf16),
            pltpu.VMEM((rows, width + 2 * PAD), bf16),
            pltpu.VMEM((2, CHUNKS, rows, chunk), bf16),
            pltpu.VMEM((bits, 2, CHUNKS, rows, chunk), bf16),
            pltpu.VMEM((bits + 1, 2, rows, PAD), f32),
            pltpu.VMEM((slots, nt, share * FINE, COARSE * rows), bf16),
            pltpu.VMEM((slots, nt, share * FINE, COARSE * rows), bf16),
            dma,
            dma((nt,)), dma((nt,)),
            dma((2,)), dma((2,)),
            dma((CHUNKS,)), dma((CHUNKS,)),
            dma((bits, CHUNKS)), dma((bits, CHUNKS)),
            dma((bits + 1,)), dma((bits + 1,)),
            dma((slots, nt)), dma((slots, nt)),
        ],
        compiler_params=pltpu.CompilerParams(collective_id=0, has_side_effects=True),
    )(traces, partners, lengths)
    found = found.reshape(share, slots, rows, LAGS)
    return jnp.transpose(found, (0, 3, 1, 2))


def solution(mesh):
    placed = (P("block", "tm"), P(), P())
    return jax.shard_map(
        functools.partial(shards, mesh.shape["block"], mesh.shape["tm"]),
        mesh=mesh,
        in_specs=placed,
        out_specs=P(("block", "tm"), None, None, None),
        check_vma=False,
    )
```

```python
import functools

import jax
import jax.numpy as jnp
from jax import lax
from jax.experimental import pallas as pl
from jax.experimental.pallas import tpu as pltpu
from jax.sharding import PartitionSpec as P

HALF = 50
ROUNDS = 2
LAGS = 101
FINE = 8
COARSE = 13
PAD = 128
CHUNKS = 8
MESH = pl.DeviceIdType.MESH


def kernel(
    nb, nt, rows, width,
    traces_ref, partners_hbm, lengths_hbm, out_ref, partners_ref, lengths_ref, table_sem,
    raw, edge, esend, erecv, ext, lhs, rhs, padded, cross, hops, norms, part, parts,
    load_sem, esend_sem, erecv_sem, hsend_sem, hrecv_sem,
    csend_sem, crecv_sem, bsend_sem, brecv_sem,
    nsend_sem, nrecv_sem, psend_sem, precv_sem,
):
    b = lax.axis_index("block")
    t = lax.axis_index("tm")
    bits = nb.bit_length() - 2
    half_mask = nb // 2
    share = rows // nt
    chunk = width // CHUNKS
    span = width + PAD
    f32, bf16 = jnp.float32, jnp.bfloat16

    def at_tm(i):
        return (b, lax.rem(t + i, nt))

    def flip(mask):
        size = 2 * mask
        low = lax.rem(b, size)
        return (b - low + lax.rem(low + mask, size), t)

    barrier = pltpu.get_barrier_semaphore()
    load = pltpu.make_async_copy(traces_ref, raw, load_sem)
    load.start()
    lengths_load = pltpu.make_async_copy(lengths_hbm, lengths_ref, table_sem.at[0])
    partners_load = pltpu.make_async_copy(partners_hbm, partners_ref, table_sem.at[1])
    lengths_load.start()
    partners_load.start()
    peers = [at_tm(i) for i in range(1, nt)] + [flip(1 << i) for i in range(bits + 1)]
    for peer in peers:
        pl.semaphore_signal(barrier, inc=1, device_id=peer, device_id_type=MESH)

    def gap(values, index, first):
        length = lengths_ref[index]
        begin = length // 2
        position = first + lax.broadcasted_iota(jnp.int32, values.shape, 1)
        recorded = (position < begin) | (position >= begin + width - length)
        return jnp.where(recorded, values, 0.0)

    lengths_load.wait()
    load.wait()
    total = jnp.zeros((rows, PAD), f32)
    for ch in range(CHUNKS):
        piece = gap(raw[:, ch * chunk : (ch + 1) * chunk], t, ch * chunk)
        cross[0, ch] = piece.astype(bf16)
        for i in range(chunk // PAD):
            tile = piece[:, i * PAD : (i + 1) * PAD]
            total = total + tile * tile
    esend[...] = total
    pl.semaphore_wait(barrier, len(peers))

    energy = []
    for i in range(1, nt):
        copy = pltpu.make_async_remote_copy(
            esend, erecv.at[i], esend_sem.at[i], erecv_sem.at[i],
            device_id=at_tm(i), device_id_type=MESH,
        )
        copy.start()
        energy.append(copy)
    to_next = pltpu.make_async_remote_copy(
        raw.at[:, pl.ds(width - PAD, PAD)], edge.at[0], hsend_sem.at[0], hrecv_sem.at[0],
        device_id=at_tm(1), device_id_type=MESH,
    )
    to_previous = pltpu.make_async_remote_copy(
        raw.at[:, pl.ds(0, PAD)], edge.at[1], hsend_sem.at[1], hrecv_sem.at[1],
        device_id=at_tm(nt - 1), device_id_type=MESH,
    )
    to_next.start()
    to_previous.start()
    crossing = []
    for ch in range(CHUNKS):
        copy = pltpu.make_async_remote_copy(
            cross.at[0, ch], cross.at[1, ch], csend_sem.at[ch], crecv_sem.at[ch],
            device_id=flip(half_mask), device_id_type=MESH,
        )
        copy.start()
        crossing.append(copy)

    summed = lengths_ref[0]
    for i in range(1, nt):
        summed = summed + lengths_ref[i]
    count = jnp.full((1, 1), summed, jnp.int32).astype(f32)
    padded[:, :PAD] = jnp.zeros((rows, PAD), bf16)
    padded[:, PAD + width :] = jnp.zeros((rows, PAD), bf16)

    for copy in energy:
        copy.wait_recv()
    for i in range(1, nt):
        total = total + erecv[i]
    power = jnp.sum(total, axis=1, keepdims=True) / count + 1e-06
    root = jnp.sqrt(power)

    def whiten(values):
        return (values / root).astype(bf16)

    norms[0, 0] = jnp.broadcast_to(1.0 / root, (rows, PAD))

    def pass_norm(stage, mask):
        copy = pltpu.make_async_remote_copy(
            norms.at[stage, 0], norms.at[stage, 1], nsend_sem.at[stage], nrecv_sem.at[stage],
            device_id=flip(mask), device_id_type=MESH,
        )
        copy.start()
        return copy

    normed = [pass_norm(0, half_mask)]
    for ch in range(CHUNKS):
        piece = whiten(gap(raw[:, ch * chunk : (ch + 1) * chunk], t, ch * chunk))
        ext[:, PAD + ch * chunk : PAD + (ch + 1) * chunk] = piece.astype(f32)
        padded[:, PAD + ch * chunk : PAD + (ch + 1) * chunk] = piece

    to_next.wait_recv()
    to_previous.wait_recv()
    before = whiten(gap(edge[0], lax.rem(t + nt - 1, nt), width - PAD)).astype(f32)
    after = whiten(gap(edge[1], lax.rem(t + 1, nt), 0)).astype(f32)
    ext[:, :PAD] = jnp.where(t > 0, before, 0.0)
    ext[:, PAD + width :] = jnp.where(t < nt - 1, after, 0.0)

    top = FINE * (COARSE - 1) - HALF
    for pair in range(rows // 2):
        both = []
        for c in (2 * pair, 2 * pair + 1):
            row = jnp.broadcast_to(ext[c : c + 1, :], (FINE, width + 2 * PAD))
            rolled = pltpu.roll(
                row, width + 2 * PAD - (PAD - top), 1, stride=1, stride_axis=0
            )
            both.append(rolled[:, :span])
        lhs[2 * FINE * pair : 2 * FINE * (pair + 1), :] = jnp.concatenate(both, axis=0).astype(bf16)

    sends = []

    def correlate(slot):
        for a in range(COARSE):
            offset = PAD - FINE * (COARSE - 1) + FINE * a
            rhs[a * rows : (a + 1) * rows, :] = padded[:, offset : offset + span]
        product = lax.dot_general(
            lhs[...], rhs[...], (((1,), (1,)), ((), ())), preferred_element_type=f32
        )
        part[slot] = product.astype(bf16).reshape(nt, share * FINE, COARSE * rows)
        for i in range(1, nt):
            copy = pltpu.make_async_remote_copy(
                part.at[slot, lax.rem(t + i, nt)], parts.at[slot, i],
                psend_sem.at[slot, i], precv_sem.at[slot, i],
                device_id=at_tm(i), device_id_type=MESH,
            )
            copy.start()
            sends.append(copy)

    correlate(0)

    partners_load.wait()
    first_mask = partners_ref[0, 0]
    second_mask = partners_ref[1, 0]
    swapped = first_mask != half_mask
    other = jnp.where(swapped, first_mask, second_mask)
    crossed = other >= half_mask

    stages = [[] for _ in range(bits)]

    def forward(stage, ch, piece):
        hops[stage, 0, ch] = piece
        copy = pltpu.make_async_remote_copy(
            hops.at[stage, 0, ch], hops.at[stage, 1, ch],
            bsend_sem.at[stage, ch], brecv_sem.at[stage, ch],
            device_id=flip(1 << stage), device_id_type=MESH,
        )
        copy.start()
        stages[stage].append(copy)

    def place(ch, piece):
        padded[:, PAD + ch * chunk : PAD + (ch + 1) * chunk] = piece

    for ch in range(CHUNKS):
        crossing[ch].wait_recv()
        arrived = cross[1, ch]
        forward(0, ch, jnp.where(crossed, arrived, cross[0, ch]))
        place(ch, arrived)
    normed[0].wait_recv()
    norms[1, 0] = jnp.where(crossed, norms[0, 1], norms[0, 0])
    normed.append(pass_norm(1, 1))
    correlate(1)
    for stage in range(bits):
        taken = lax.rem(other // (1 << stage), 2) == 1
        for ch in range(CHUNKS):
            stages[stage][ch].wait_recv()
            piece = jnp.where(taken, hops[stage, 1, ch], hops[stage, 0, ch])
            if stage < bits - 1:
                forward(stage + 1, ch, piece)
            else:
                place(ch, piece)
        if stage < bits - 1:
            normed[stage + 1].wait_recv()
            norms[stage + 2, 0] = jnp.where(taken, norms[stage + 1, 1], norms[stage + 1, 0])
            normed.append(pass_norm(stage + 2, 2 << stage))
    correlate(2)

    scale = 1.0 / jnp.sqrt(count)
    full = COARSE * rows // PAD
    quad = PAD // rows
    lane = lax.broadcasted_iota(jnp.int32, (full * FINE, PAD), 1)

    def gathered(slot):
        mine = part[slot, t].astype(f32)
        for i in range(1, nt):
            sends[slot * (nt - 1) + i - 1].wait_recv()
            mine = mine + parts[slot, i].astype(f32)
        mine = mine * scale
        out = []
        for c0 in range(0, share, quad):
            blocks = []
            rests = []
            for c in range(c0, min(c0 + quad, share)):
                own = mine[c * FINE : (c + 1) * FINE]
                blocks.append(jnp.concatenate(
                    [own[:, j * PAD : (j + 1) * PAD] for j in range(full)], axis=0
                ))
                rests.append(own[:, full * PAD :])
            real = len(blocks)
            blocks += [jnp.zeros((full * FINE, PAD), f32)] * (quad - real)
            step = 1
            while step < quad:
                odd = lax.rem(lane // (rows * step), 2) == 1
                for i in range(quad):
                    if not i & step:
                        one, two = blocks[i], blocks[i + step]
                        blocks[i] = jnp.where(odd, pltpu.roll(two, rows * step, 1), one)
                        blocks[i + step] = jnp.where(odd, two, pltpu.roll(one, PAD - rows * step, 1))
                step *= 2
            lags = [
                blocks[i][j * FINE : (j + 1) * FINE] for j in range(full) for i in range(quad)
            ]
            if real < quad:
                rests.append(jnp.zeros((FINE, PAD - real * rows), f32))
            lags.append(jnp.concatenate(rests, axis=1))
            lags.append(jnp.zeros((PAD - FINE * COARSE, PAD), f32))
            turned = jnp.concatenate(lags, axis=0).T
            out.append(turned.reshape(quad, rows, PAD)[:real])
        return jnp.concatenate(out, axis=0)

    shape = (share, rows, PAD)
    index, column, lag = (lax.broadcasted_iota(jnp.int32, shape, i) for i in range(3))
    killed = (lag == HALF) & (column == t * share + index)
    out_ref[:, :rows, :] = jnp.where(killed, 0.0, gathered(0))[:, :, :LAGS]
    near = gathered(1) * norms[0, 1][None]
    normed[bits].wait_recv()
    factor = jnp.where(taken, norms[bits, 1], norms[bits, 0])
    far = gathered(2) * factor[None]
    out_ref[:, rows : 2 * rows, :] = jnp.where(swapped, far, near)[:, :, :LAGS]
    out_ref[:, 2 * rows :, :] = jnp.where(swapped, near, far)[:, :, :LAGS]

    for copy in energy + [to_next, to_previous] + crossing + sum(stages, []) + normed + sends:
        copy.wait_send()


def shards(nb, nt, traces, partners, lengths):
    rows, width = traces.shape
    share = rows // nt
    bits = nb.bit_length() - 2
    chunk = width // CHUNKS
    span = width + PAD
    f32, bf16 = jnp.float32, jnp.bfloat16
    dma = pltpu.SemaphoreType.DMA
    slots = ROUNDS + 1
    found = pl.pallas_call(
        functools.partial(kernel, nb, nt, rows, width),
        out_shape=pltpu.VMEM((share, slots * rows, LAGS), f32),
        in_specs=[
            pl.BlockSpec(memory_space=pl.ANY),
            pl.BlockSpec(memory_space=pl.ANY),
            pl.BlockSpec(memory_space=pl.ANY),
        ],
        out_specs=pl.BlockSpec(memory_space=pltpu.VMEM),
        scratch_shapes=[
            pltpu.SMEM(partners.shape, jnp.int32),
            pltpu.SMEM(lengths.shape, jnp.int32),
            dma((2,)),
            pltpu.VMEM((rows, width), f32),
            pltpu.VMEM((2, rows, PAD), f32),
            pltpu.VMEM((rows, PAD), f32),
            pltpu.VMEM((nt, rows, PAD), f32),
            pltpu.VMEM((rows, width + 2 * PAD), f32),
            pltpu.VMEM((rows * FINE, span), bf16),
            pltpu.VMEM((COARSE * rows, span), bf16),
            pltpu.VMEM((rows, width + 2 * PAD), bf16),
            pltpu.VMEM((2, CHUNKS, rows, chunk), bf16),
            pltpu.VMEM((bits, 2, CHUNKS, rows, chunk), bf16),
            pltpu.VMEM((bits + 1, 2, rows, PAD), f32),
            pltpu.VMEM((slots, nt, share * FINE, COARSE * rows), bf16),
            pltpu.VMEM((slots, nt, share * FINE, COARSE * rows), bf16),
            dma,
            dma((nt,)), dma((nt,)),
            dma((2,)), dma((2,)),
            dma((CHUNKS,)), dma((CHUNKS,)),
            dma((bits, CHUNKS)), dma((bits, CHUNKS)),
            dma((bits + 1,)), dma((bits + 1,)),
            dma((slots, nt)), dma((slots, nt)),
        ],
        compiler_params=pltpu.CompilerParams(collective_id=0, has_side_effects=True),
    )(traces, partners, lengths)
    found = found.reshape(share, slots, rows, LAGS)
    return jnp.transpose(found, (0, 3, 1, 2))


def solution(mesh):
    placed = (P("block", "tm"), P(), P())
    return jax.shard_map(
        functools.partial(shards, mesh.shape["block"], mesh.shape["tm"]),
        mesh=mesh,
        in_specs=placed,
        out_specs=P(("block", "tm"), None, None, None),
        check_vma=False,
    )
```

```python
import functools

import jax
import jax.numpy as jnp
from jax import lax
from jax.experimental import pallas as pl
from jax.experimental.pallas import tpu as pltpu
from jax.sharding import PartitionSpec as P

HALF = 50
ROUNDS = 2
LAGS = 101
FINE = 8
COARSE = 13
PAD = 128
CHUNKS = 8
STOPS = (3, 5, 7)
MESH = pl.DeviceIdType.MESH


def kernel(
    nb, nt, rows, width,
    traces_ref, partners_hbm, lengths_hbm, out_ref, partners_ref, lengths_ref, table_sem,
    raw, edge, esend, erecv, ext, lhs, rhs, padded, cross, hops, norms, part, parts,
    load_sem, esend_sem, erecv_sem, hsend_sem, hrecv_sem,
    csend_sem, crecv_sem, bsend_sem, brecv_sem,
    nsend_sem, nrecv_sem, psend_sem, precv_sem,
):
    b = lax.axis_index("block")
    t = lax.axis_index("tm")
    bits = nb.bit_length() - 2
    half_mask = nb // 2
    share = rows // nt
    chunk = width // CHUNKS
    span = width + PAD
    f32, bf16 = jnp.float32, jnp.bfloat16

    def at_tm(i):
        return (b, lax.rem(t + i, nt))

    def flip(mask):
        size = 2 * mask
        low = lax.rem(b, size)
        return (b - low + lax.rem(low + mask, size), t)

    barrier = pltpu.get_barrier_semaphore()
    peers = [flip(1 << i) for i in range(bits, -1, -1)] + [at_tm(i) for i in range(1, nt)]
    for peer in peers:
        pl.semaphore_signal(barrier, inc=1, device_id=peer, device_id_type=MESH)

    load = pltpu.make_async_copy(traces_ref, raw, load_sem)
    load.start()
    lengths_load = pltpu.make_async_copy(lengths_hbm, lengths_ref, table_sem.at[0])
    partners_load = pltpu.make_async_copy(partners_hbm, partners_ref, table_sem.at[1])
    lengths_load.start()
    partners_load.start()
    def gap(values, index, first):
        length = lengths_ref[index]
        begin = length // 2
        position = first + lax.broadcasted_iota(jnp.int32, values.shape, 1)
        recorded = (position < begin) | (position >= begin + width - length)
        return jnp.where(recorded, values, 0.0)

    lengths_load.wait()
    load.wait()
    total = jnp.zeros((rows, PAD), f32)
    for ch in range(CHUNKS):
        piece = gap(raw[:, ch * chunk : (ch + 1) * chunk], t, ch * chunk)
        cross[0, ch] = piece.astype(bf16)
        for i in range(chunk // PAD):
            tile = piece[:, i * PAD : (i + 1) * PAD]
            total = total + tile * tile
    esend[...] = total
    pl.semaphore_wait(barrier, len(peers))

    energy = []
    for i in range(1, nt):
        copy = pltpu.make_async_remote_copy(
            esend, erecv.at[i], esend_sem.at[i], erecv_sem.at[i],
            device_id=at_tm(i), device_id_type=MESH,
        )
        copy.start()
        energy.append(copy)
    to_next = pltpu.make_async_remote_copy(
        raw.at[:, pl.ds(width - PAD, PAD)], edge.at[0], hsend_sem.at[0], hrecv_sem.at[0],
        device_id=at_tm(1), device_id_type=MESH,
    )
    to_previous = pltpu.make_async_remote_copy(
        raw.at[:, pl.ds(0, PAD)], edge.at[1], hsend_sem.at[1], hrecv_sem.at[1],
        device_id=at_tm(nt - 1), device_id_type=MESH,
    )
    to_next.start()
    to_previous.start()
    crossing = []
    for ch in range(CHUNKS):
        copy = pltpu.make_async_remote_copy(
            cross.at[0, ch], cross.at[1, ch], csend_sem.at[ch], crecv_sem.at[ch],
            device_id=flip(half_mask), device_id_type=MESH,
        )
        copy.start()
        crossing.append(copy)

    summed = lengths_ref[0]
    for i in range(1, nt):
        summed = summed + lengths_ref[i]
    count = jnp.full((1, 1), summed, jnp.int32).astype(f32)
    padded[:, :PAD] = jnp.zeros((rows, PAD), bf16)
    padded[:, PAD + width :] = jnp.zeros((rows, PAD), bf16)

    for copy in energy:
        copy.wait_recv()
    for i in range(1, nt):
        total = total + erecv[i]
    power = jnp.sum(total, axis=1, keepdims=True) / count + 1e-06
    root = jnp.sqrt(power)

    def whiten(values):
        return (values / root).astype(bf16)

    norms[0, 0] = jnp.broadcast_to(1.0 / root, (rows, PAD))

    def pass_norm(stage, mask):
        copy = pltpu.make_async_remote_copy(
            norms.at[stage, 0], norms.at[stage, 1], nsend_sem.at[stage], nrecv_sem.at[stage],
            device_id=flip(mask), device_id_type=MESH,
        )
        copy.start()
        return copy

    normed = [pass_norm(0, half_mask)]
    for ch in range(CHUNKS):
        piece = whiten(gap(raw[:, ch * chunk : (ch + 1) * chunk], t, ch * chunk))
        ext[:, PAD + ch * chunk : PAD + (ch + 1) * chunk] = piece.astype(f32)
        padded[:, PAD + ch * chunk : PAD + (ch + 1) * chunk] = piece

    to_next.wait_recv()
    to_previous.wait_recv()
    before = whiten(gap(edge[0], lax.rem(t + nt - 1, nt), width - PAD)).astype(f32)
    after = whiten(gap(edge[1], lax.rem(t + 1, nt), 0)).astype(f32)
    ext[:, :PAD] = jnp.where(t > 0, before, 0.0)
    ext[:, PAD + width :] = jnp.where(t < nt - 1, after, 0.0)

    top = FINE * (COARSE - 1) - HALF
    for pair in range(rows // 2):
        both = []
        for c in (2 * pair, 2 * pair + 1):
            row = jnp.broadcast_to(ext[c : c + 1, :], (FINE, width + 2 * PAD))
            rolled = pltpu.roll(
                row, width + 2 * PAD - (PAD - top), 1, stride=1, stride_axis=0
            )
            both.append(rolled[:, :span])
        lhs[2 * FINE * pair : 2 * FINE * (pair + 1), :] = jnp.concatenate(both, axis=0).astype(bf16)

    sends = []

    def multiply(first, last):
        for a in range(COARSE):
            offset = PAD - FINE * (COARSE - 1) + FINE * a
            rhs[a * rows : (a + 1) * rows, first:last] = padded[:, offset + first : offset + last]
        return lax.dot_general(
            lhs[:, first:last], rhs[:, first:last],
            (((1,), (1,)), ((), ())), preferred_element_type=f32,
        )

    def correlate(slot):
        scatter(slot, multiply(0, span))

    def scatter(slot, product):
        part[slot] = product.astype(bf16).reshape(nt, share * FINE, COARSE * rows)
        for i in range(1, nt):
            copy = pltpu.make_async_remote_copy(
                part.at[slot, lax.rem(t + i, nt)], parts.at[slot, i],
                psend_sem.at[slot, i], precv_sem.at[slot, i],
                device_id=at_tm(i), device_id_type=MESH,
            )
            copy.start()
            sends.append(copy)

    correlate(0)

    partners_load.wait()
    first_mask = partners_ref[0, 0]
    second_mask = partners_ref[1, 0]
    swapped = first_mask != half_mask
    other = jnp.where(swapped, first_mask, second_mask)
    crossed = other >= half_mask

    ends = [0]
    pieces = []
    stages = [[] for _ in range(bits)]

    def forward(stage, ch, piece):
        hops[stage, 0, ch] = piece
        copy = pltpu.make_async_remote_copy(
            hops.at[stage, 0, ch], hops.at[stage, 1, ch],
            bsend_sem.at[stage, ch], brecv_sem.at[stage, ch],
            device_id=flip(1 << stage), device_id_type=MESH,
        )
        copy.start()
        stages[stage].append(copy)

    def place(ch, piece):
        padded[:, PAD + ch * chunk : PAD + (ch + 1) * chunk] = piece

    for ch in range(CHUNKS):
        crossing[ch].wait_recv()
        arrived = cross[1, ch]
        forward(0, ch, jnp.where(crossed, arrived, cross[0, ch]))
        place(ch, arrived)
    normed[0].wait_recv()
    norms[1, 0] = jnp.where(crossed, norms[0, 1], norms[0, 0])
    normed.append(pass_norm(1, 1))
    correlate(1)
    for stage in range(bits):
        taken = lax.rem(other // (1 << stage), 2) == 1
        for ch in range(CHUNKS):
            stages[stage][ch].wait_recv()
            piece = jnp.where(taken, hops[stage, 1, ch], hops[stage, 0, ch])
            if stage < bits - 1:
                forward(stage + 1, ch, piece)
            else:
                place(ch, piece)
                if ch in STOPS:
                    done = ends[-1]
                    ends.append(span if ch == CHUNKS - 1 else (ch + 1) * chunk)
                    pieces.append(multiply(done, ends[-1]))
        if stage < bits - 1:
            normed[stage + 1].wait_recv()
            norms[stage + 2, 0] = jnp.where(taken, norms[stage + 1, 1], norms[stage + 1, 0])
            normed.append(pass_norm(stage + 2, 2 << stage))
    scatter(2, functools.reduce(jnp.add, pieces))

    scale = 1.0 / jnp.sqrt(count)
    full = COARSE * rows // PAD
    quad = PAD // rows
    lane = lax.broadcasted_iota(jnp.int32, (full * FINE, PAD), 1)

    def gathered(slot):
        mine = part[slot, t].astype(f32)
        for i in range(1, nt):
            sends[slot * (nt - 1) + i - 1].wait_recv()
            mine = mine + parts[slot, i].astype(f32)
        mine = mine * scale
        out = []
        for c0 in range(0, share, quad):
            blocks = []
            rests = []
            for c in range(c0, min(c0 + quad, share)):
                own = mine[c * FINE : (c + 1) * FINE]
                blocks.append(jnp.concatenate(
                    [own[:, j * PAD : (j + 1) * PAD] for j in range(full)], axis=0
                ))
                rests.append(own[:, full * PAD :])
            real = len(blocks)
            blocks += [jnp.zeros((full * FINE, PAD), f32)] * (quad - real)
            step = 1
            while step < quad:
                odd = lax.rem(lane // (rows * step), 2) == 1
                for i in range(quad):
                    if not i & step:
                        one, two = blocks[i], blocks[i + step]
                        blocks[i] = jnp.where(odd, pltpu.roll(two, rows * step, 1), one)
                        blocks[i + step] = jnp.where(odd, two, pltpu.roll(one, PAD - rows * step, 1))
                step *= 2
            lags = [
                blocks[i][j * FINE : (j + 1) * FINE] for j in range(full) for i in range(quad)
            ]
            if real < quad:
                rests.append(jnp.zeros((FINE, PAD - real * rows), f32))
            lags.append(jnp.concatenate(rests, axis=1))
            lags.append(jnp.zeros((PAD - FINE * COARSE, PAD), f32))
            turned = jnp.concatenate(lags, axis=0).T
            out.append(turned.reshape(quad, rows, PAD)[:real])
        return jnp.concatenate(out, axis=0)

    shape = (share, rows, PAD)
    index, column, lag = (lax.broadcasted_iota(jnp.int32, shape, i) for i in range(3))
    killed = (lag == HALF) & (column == t * share + index)
    out_ref[:, :rows, :] = jnp.where(killed, 0.0, gathered(0))[:, :, :LAGS]
    near = gathered(1) * norms[0, 1][None]
    normed[bits].wait_recv()
    factor = jnp.where(taken, norms[bits, 1], norms[bits, 0])
    far = gathered(2) * factor[None]
    out_ref[:, rows : 2 * rows, :] = jnp.where(swapped, far, near)[:, :, :LAGS]
    out_ref[:, 2 * rows :, :] = jnp.where(swapped, near, far)[:, :, :LAGS]

    for copy in energy + [to_next, to_previous] + crossing + sum(stages, []) + normed + sends:
        copy.wait_send()


def shards(nb, nt, traces, partners, lengths):
    rows, width = traces.shape
    share = rows // nt
    bits = nb.bit_length() - 2
    chunk = width // CHUNKS
    span = width + PAD
    f32, bf16 = jnp.float32, jnp.bfloat16
    dma = pltpu.SemaphoreType.DMA
    slots = ROUNDS + 1
    found = pl.pallas_call(
        functools.partial(kernel, nb, nt, rows, width),
        out_shape=pltpu.VMEM((share, slots * rows, LAGS), f32),
        in_specs=[
            pl.BlockSpec(memory_space=pl.ANY),
            pl.BlockSpec(memory_space=pl.ANY),
            pl.BlockSpec(memory_space=pl.ANY),
        ],
        out_specs=pl.BlockSpec(memory_space=pltpu.VMEM),
        scratch_shapes=[
            pltpu.SMEM(partners.shape, jnp.int32),
            pltpu.SMEM(lengths.shape, jnp.int32),
            dma((2,)),
            pltpu.VMEM((rows, width), f32),
            pltpu.VMEM((2, rows, PAD), f32),
            pltpu.VMEM((rows, PAD), f32),
            pltpu.VMEM((nt, rows, PAD), f32),
            pltpu.VMEM((rows, width + 2 * PAD), f32),
            pltpu.VMEM((rows * FINE, span), bf16),
            pltpu.VMEM((COARSE * rows, span), bf16),
            pltpu.VMEM((rows, width + 2 * PAD), bf16),
            pltpu.VMEM((2, CHUNKS, rows, chunk), bf16),
            pltpu.VMEM((bits, 2, CHUNKS, rows, chunk), bf16),
            pltpu.VMEM((bits + 1, 2, rows, PAD), f32),
            pltpu.VMEM((slots, nt, share * FINE, COARSE * rows), bf16),
            pltpu.VMEM((slots, nt, share * FINE, COARSE * rows), bf16),
            dma,
            dma((nt,)), dma((nt,)),
            dma((2,)), dma((2,)),
            dma((CHUNKS,)), dma((CHUNKS,)),
            dma((bits, CHUNKS)), dma((bits, CHUNKS)),
            dma((bits + 1,)), dma((bits + 1,)),
            dma((slots, nt)), dma((slots, nt)),
        ],
        compiler_params=pltpu.CompilerParams(collective_id=0, has_side_effects=True),
    )(traces, partners, lengths)
    found = found.reshape(share, slots, rows, LAGS)
    return jnp.transpose(found, (0, 3, 1, 2))


def solution(mesh):
    placed = (P("block", "tm"), P(), P())
    return jax.shard_map(
        functools.partial(shards, mesh.shape["block"], mesh.shape["tm"]),
        mesh=mesh,
        in_specs=placed,
        out_specs=P(("block", "tm"), None, None, None),
        check_vma=False,
    )
```

```python
import functools

import jax
import jax.numpy as jnp
from jax import lax
from jax.experimental import pallas as pl
from jax.experimental.pallas import tpu as pltpu
from jax.sharding import PartitionSpec as P

HALF = 50
ROUNDS = 2
LAGS = 101
FINE = 8
COARSE = 13
PAD = 128
CHUNKS = 8
STOPS = (1, 3, 5, 7)
MESH = pl.DeviceIdType.MESH


def kernel(
    nb, nt, rows, width,
    traces_ref, partners_hbm, lengths_hbm, out_ref, partners_ref, lengths_ref, table_sem,
    raw, edge, esend, erecv, ext, lhs, rhs, padded, cross, hops, norms, part, parts,
    load_sem, esend_sem, erecv_sem, hsend_sem, hrecv_sem,
    csend_sem, crecv_sem, bsend_sem, brecv_sem,
    nsend_sem, nrecv_sem, psend_sem, precv_sem,
):
    b = lax.axis_index("block")
    t = lax.axis_index("tm")
    bits = nb.bit_length() - 2
    half_mask = nb // 2
    share = rows // nt
    chunk = width // CHUNKS
    span = width + PAD
    f32, bf16 = jnp.float32, jnp.bfloat16

    def at_tm(i):
        return (b, lax.rem(t + i, nt))

    def flip(mask):
        size = 2 * mask
        low = lax.rem(b, size)
        return (b - low + lax.rem(low + mask, size), t)

    barrier = pltpu.get_barrier_semaphore()
    peers = [flip(1 << i) for i in range(bits, -1, -1)] + [at_tm(i) for i in range(1, nt)]
    for peer in peers:
        pl.semaphore_signal(barrier, inc=1, device_id=peer, device_id_type=MESH)

    load = pltpu.make_async_copy(traces_ref, raw, load_sem)
    load.start()
    lengths_load = pltpu.make_async_copy(lengths_hbm, lengths_ref, table_sem.at[0])
    partners_load = pltpu.make_async_copy(partners_hbm, partners_ref, table_sem.at[1])
    lengths_load.start()
    partners_load.start()
    def gap(values, index, first):
        length = lengths_ref[index]
        begin = length // 2
        position = first + lax.broadcasted_iota(jnp.int32, values.shape, 1)
        recorded = (position < begin) | (position >= begin + width - length)
        return jnp.where(recorded, values, 0.0)

    lengths_load.wait()
    load.wait()
    total = jnp.zeros((rows, PAD), f32)
    for ch in range(CHUNKS):
        piece = gap(raw[:, ch * chunk : (ch + 1) * chunk], t, ch * chunk)
        cross[0, ch] = piece.astype(bf16)
        for i in range(chunk // PAD):
            tile = piece[:, i * PAD : (i + 1) * PAD]
            total = total + tile * tile
    esend[...] = total
    pl.semaphore_wait(barrier, len(peers))

    energy = []
    for i in range(1, nt):
        copy = pltpu.make_async_remote_copy(
            esend, erecv.at[i], esend_sem.at[i], erecv_sem.at[i],
            device_id=at_tm(i), device_id_type=MESH,
        )
        copy.start()
        energy.append(copy)
    to_next = pltpu.make_async_remote_copy(
        raw.at[:, pl.ds(width - PAD, PAD)], edge.at[0], hsend_sem.at[0], hrecv_sem.at[0],
        device_id=at_tm(1), device_id_type=MESH,
    )
    to_previous = pltpu.make_async_remote_copy(
        raw.at[:, pl.ds(0, PAD)], edge.at[1], hsend_sem.at[1], hrecv_sem.at[1],
        device_id=at_tm(nt - 1), device_id_type=MESH,
    )
    to_next.start()
    to_previous.start()
    crossing = []
    for ch in range(CHUNKS):
        copy = pltpu.make_async_remote_copy(
            cross.at[0, ch], cross.at[1, ch], csend_sem.at[ch], crecv_sem.at[ch],
            device_id=flip(half_mask), device_id_type=MESH,
        )
        copy.start()
        crossing.append(copy)

    summed = lengths_ref[0]
    for i in range(1, nt):
        summed = summed + lengths_ref[i]
    count = jnp.full((1, 1), summed, jnp.int32).astype(f32)
    padded[:, :PAD] = jnp.zeros((rows, PAD), bf16)
    padded[:, PAD + width :] = jnp.zeros((rows, PAD), bf16)

    for copy in energy:
        copy.wait_recv()
    for i in range(1, nt):
        total = total + erecv[i]
    power = jnp.sum(total, axis=1, keepdims=True) / count + 1e-06
    root = jnp.sqrt(power)

    def whiten(values):
        return (values / root).astype(bf16)

    norms[0, 0] = jnp.broadcast_to(1.0 / root, (rows, PAD))

    def pass_norm(stage, mask):
        copy = pltpu.make_async_remote_copy(
            norms.at[stage, 0], norms.at[stage, 1], nsend_sem.at[stage], nrecv_sem.at[stage],
            device_id=flip(mask), device_id_type=MESH,
        )
        copy.start()
        return copy

    normed = [pass_norm(0, half_mask)]
    for ch in range(CHUNKS):
        piece = whiten(gap(raw[:, ch * chunk : (ch + 1) * chunk], t, ch * chunk))
        ext[:, PAD + ch * chunk : PAD + (ch + 1) * chunk] = piece.astype(f32)
        padded[:, PAD + ch * chunk : PAD + (ch + 1) * chunk] = piece

    to_next.wait_recv()
    to_previous.wait_recv()
    before = whiten(gap(edge[0], lax.rem(t + nt - 1, nt), width - PAD)).astype(f32)
    after = whiten(gap(edge[1], lax.rem(t + 1, nt), 0)).astype(f32)
    ext[:, :PAD] = jnp.where(t > 0, before, 0.0)
    ext[:, PAD + width :] = jnp.where(t < nt - 1, after, 0.0)

    top = FINE * (COARSE - 1) - HALF
    for pair in range(rows // 2):
        both = []
        for c in (2 * pair, 2 * pair + 1):
            row = jnp.broadcast_to(ext[c : c + 1, :], (FINE, width + 2 * PAD))
            rolled = pltpu.roll(
                row, width + 2 * PAD - (PAD - top), 1, stride=1, stride_axis=0
            )
            both.append(rolled[:, :span])
        lhs[2 * FINE * pair : 2 * FINE * (pair + 1), :] = jnp.concatenate(both, axis=0).astype(bf16)

    sends = []

    def multiply(first, last):
        for a in range(COARSE):
            offset = PAD - FINE * (COARSE - 1) + FINE * a
            rhs[a * rows : (a + 1) * rows, first:last] = padded[:, offset + first : offset + last]
        return lax.dot_general(
            lhs[:, first:last], rhs[:, first:last],
            (((1,), (1,)), ((), ())), preferred_element_type=f32,
        )

    def correlate(slot):
        scatter(slot, multiply(0, span))

    def scatter(slot, product):
        part[slot] = product.astype(bf16).reshape(nt, share * FINE, COARSE * rows)
        for i in range(1, nt):
            copy = pltpu.make_async_remote_copy(
                part.at[slot, lax.rem(t + i, nt)], parts.at[slot, i],
                psend_sem.at[slot, i], precv_sem.at[slot, i],
                device_id=at_tm(i), device_id_type=MESH,
            )
            copy.start()
            sends.append(copy)

    correlate(0)

    partners_load.wait()
    first_mask = partners_ref[0, 0]
    second_mask = partners_ref[1, 0]
    swapped = first_mask != half_mask
    other = jnp.where(swapped, first_mask, second_mask)
    crossed = other >= half_mask

    ends = [0]
    pieces = []
    stages = [[] for _ in range(bits)]

    def forward(stage, ch, piece):
        hops[stage, 0, ch] = piece
        copy = pltpu.make_async_remote_copy(
            hops.at[stage, 0, ch], hops.at[stage, 1, ch],
            bsend_sem.at[stage, ch], brecv_sem.at[stage, ch],
            device_id=flip(1 << stage), device_id_type=MESH,
        )
        copy.start()
        stages[stage].append(copy)

    def place(ch, piece):
        padded[:, PAD + ch * chunk : PAD + (ch + 1) * chunk] = piece

    for ch in range(CHUNKS):
        crossing[ch].wait_recv()
        arrived = cross[1, ch]
        forward(0, ch, jnp.where(crossed, arrived, cross[0, ch]))
        place(ch, arrived)
    normed[0].wait_recv()
    norms[1, 0] = jnp.where(crossed, norms[0, 1], norms[0, 0])
    normed.append(pass_norm(1, 1))
    correlate(1)
    for stage in range(bits):
        taken = lax.rem(other // (1 << stage), 2) == 1
        for ch in range(CHUNKS):
            stages[stage][ch].wait_recv()
            piece = jnp.where(taken, hops[stage, 1, ch], hops[stage, 0, ch])
            if stage < bits - 1:
                forward(stage + 1, ch, piece)
            else:
                place(ch, piece)
                if ch in STOPS:
                    done = ends[-1]
                    ends.append(span if ch == CHUNKS - 1 else (ch + 1) * chunk)
                    pieces.append(multiply(done, ends[-1]))
        if stage < bits - 1:
            normed[stage + 1].wait_recv()
            norms[stage + 2, 0] = jnp.where(taken, norms[stage + 1, 1], norms[stage + 1, 0])
            normed.append(pass_norm(stage + 2, 2 << stage))
    scatter(2, functools.reduce(jnp.add, pieces))

    scale = 1.0 / jnp.sqrt(count)
    full = COARSE * rows // PAD
    quad = PAD // rows
    lane = lax.broadcasted_iota(jnp.int32, (full * FINE, PAD), 1)

    def gathered(slot):
        mine = part[slot, t].astype(f32)
        for i in range(1, nt):
            sends[slot * (nt - 1) + i - 1].wait_recv()
            mine = mine + parts[slot, i].astype(f32)
        mine = mine * scale
        out = []
        for c0 in range(0, share, quad):
            blocks = []
            rests = []
            for c in range(c0, min(c0 + quad, share)):
                own = mine[c * FINE : (c + 1) * FINE]
                blocks.append(jnp.concatenate(
                    [own[:, j * PAD : (j + 1) * PAD] for j in range(full)], axis=0
                ))
                rests.append(own[:, full * PAD :])
            real = len(blocks)
            blocks += [jnp.zeros((full * FINE, PAD), f32)] * (quad - real)
            step = 1
            while step < quad:
                odd = lax.rem(lane // (rows * step), 2) == 1
                for i in range(quad):
                    if not i & step:
                        one, two = blocks[i], blocks[i + step]
                        blocks[i] = jnp.where(odd, pltpu.roll(two, rows * step, 1), one)
                        blocks[i + step] = jnp.where(odd, two, pltpu.roll(one, PAD - rows * step, 1))
                step *= 2
            lags = [
                blocks[i][j * FINE : (j + 1) * FINE] for j in range(full) for i in range(quad)
            ]
            if real < quad:
                rests.append(jnp.zeros((FINE, PAD - real * rows), f32))
            lags.append(jnp.concatenate(rests, axis=1))
            lags.append(jnp.zeros((PAD - FINE * COARSE, PAD), f32))
            turned = jnp.concatenate(lags, axis=0).T
            out.append(turned.reshape(quad, rows, PAD)[:real])
        return jnp.concatenate(out, axis=0)

    shape = (share, rows, PAD)
    index, column, lag = (lax.broadcasted_iota(jnp.int32, shape, i) for i in range(3))
    killed = (lag == HALF) & (column == t * share + index)
    out_ref[:, :rows, :] = jnp.where(killed, 0.0, gathered(0))[:, :, :LAGS]
    near = gathered(1) * norms[0, 1][None]
    normed[bits].wait_recv()
    factor = jnp.where(taken, norms[bits, 1], norms[bits, 0])
    far = gathered(2) * factor[None]
    out_ref[:, rows : 2 * rows, :] = jnp.where(swapped, far, near)[:, :, :LAGS]
    out_ref[:, 2 * rows :, :] = jnp.where(swapped, near, far)[:, :, :LAGS]

    for copy in energy + [to_next, to_previous] + crossing + sum(stages, []) + normed + sends:
        copy.wait_send()


def shards(nb, nt, traces, partners, lengths):
    rows, width = traces.shape
    share = rows // nt
    bits = nb.bit_length() - 2
    chunk = width // CHUNKS
    span = width + PAD
    f32, bf16 = jnp.float32, jnp.bfloat16
    dma = pltpu.SemaphoreType.DMA
    slots = ROUNDS + 1
    found = pl.pallas_call(
        functools.partial(kernel, nb, nt, rows, width),
        out_shape=pltpu.VMEM((share, slots * rows, LAGS), f32),
        in_specs=[
            pl.BlockSpec(memory_space=pl.ANY),
            pl.BlockSpec(memory_space=pl.ANY),
            pl.BlockSpec(memory_space=pl.ANY),
        ],
        out_specs=pl.BlockSpec(memory_space=pltpu.VMEM),
        scratch_shapes=[
            pltpu.SMEM(partners.shape, jnp.int32),
            pltpu.SMEM(lengths.shape, jnp.int32),
            dma((2,)),
            pltpu.VMEM((rows, width), f32),
            pltpu.VMEM((2, rows, PAD), f32),
            pltpu.VMEM((rows, PAD), f32),
            pltpu.VMEM((nt, rows, PAD), f32),
            pltpu.VMEM((rows, width + 2 * PAD), f32),
            pltpu.VMEM((rows * FINE, span), bf16),
            pltpu.VMEM((COARSE * rows, span), bf16),
            pltpu.VMEM((rows, width + 2 * PAD), bf16),
            pltpu.VMEM((2, CHUNKS, rows, chunk), bf16),
            pltpu.VMEM((bits, 2, CHUNKS, rows, chunk), bf16),
            pltpu.VMEM((bits + 1, 2, rows, PAD), f32),
            pltpu.VMEM((slots, nt, share * FINE, COARSE * rows), bf16),
            pltpu.VMEM((slots, nt, share * FINE, COARSE * rows), bf16),
            dma,
            dma((nt,)), dma((nt,)),
            dma((2,)), dma((2,)),
            dma((CHUNKS,)), dma((CHUNKS,)),
            dma((bits, CHUNKS)), dma((bits, CHUNKS)),
            dma((bits + 1,)), dma((bits + 1,)),
            dma((slots, nt)), dma((slots, nt)),
        ],
        compiler_params=pltpu.CompilerParams(collective_id=0, has_side_effects=True),
    )(traces, partners, lengths)
    found = found.reshape(share, slots, rows, LAGS)
    return jnp.transpose(found, (0, 3, 1, 2))


def solution(mesh):
    placed = (P("block", "tm"), P(), P())
    return jax.shard_map(
        functools.partial(shards, mesh.shape["block"], mesh.shape["tm"]),
        mesh=mesh,
        in_specs=placed,
        out_specs=P(("block", "tm"), None, None, None),
        check_vma=False,
    )
```

```python
import functools

import jax
import jax.numpy as jnp
from jax import lax
from jax.experimental import pallas as pl
from jax.experimental.pallas import tpu as pltpu
from jax.sharding import PartitionSpec as P

HALF = 50
ROUNDS = 2
LAGS = 101
FINE = 8
COARSE = 13
PAD = 128
CHUNKS = 8
STOPS = (1, 3, 5, 7)
MESH = pl.DeviceIdType.MESH


def kernel(
    nb, nt, rows, width,
    traces_ref, partners_hbm, lengths_hbm, out_ref, partners_ref, lengths_ref, table_sem,
    raw, edge, esend, erecv, ext, lhs, rhs, padded, cross, hops, norms, part, parts,
    load_sem, esend_sem, erecv_sem, hsend_sem, hrecv_sem,
    csend_sem, crecv_sem, bsend_sem, brecv_sem,
    nsend_sem, nrecv_sem, psend_sem, precv_sem,
):
    b = lax.axis_index("block")
    t = lax.axis_index("tm")
    bits = nb.bit_length() - 2
    half_mask = nb // 2
    share = rows // nt
    chunk = width // CHUNKS
    span = width + PAD
    f32, bf16 = jnp.float32, jnp.bfloat16

    def at_tm(i):
        return (b, lax.rem(t + i, nt))

    def flip(mask):
        size = 2 * mask
        low = lax.rem(b, size)
        return (b - low + lax.rem(low + mask, size), t)

    barrier = pltpu.get_barrier_semaphore()
    peers = [flip(1 << i) for i in range(bits, -1, -1)] + [at_tm(i) for i in range(1, nt)]
    for peer in peers:
        pl.semaphore_signal(barrier, inc=1, device_id=peer, device_id_type=MESH)

    load = pltpu.make_async_copy(traces_ref, raw, load_sem)
    load.start()
    lengths_load = pltpu.make_async_copy(lengths_hbm, lengths_ref, table_sem.at[0])
    partners_load = pltpu.make_async_copy(partners_hbm, partners_ref, table_sem.at[1])
    lengths_load.start()
    partners_load.start()
    def gap(values, index, first):
        length = lengths_ref[index]
        begin = length // 2
        position = first + lax.broadcasted_iota(jnp.int32, values.shape, 1)
        recorded = (position < begin) | (position >= begin + width - length)
        return jnp.where(recorded, values, 0.0)

    lengths_load.wait()
    load.wait()
    crossing = []
    for ch in range(CHUNKS):
        piece = gap(raw[:, ch * chunk : (ch + 1) * chunk], t, ch * chunk)
        cross[0, ch] = piece.astype(bf16)
        if ch == 0:
            pl.semaphore_wait(barrier, len(peers))
        copy = pltpu.make_async_remote_copy(
            cross.at[0, ch], cross.at[1, ch], csend_sem.at[ch], crecv_sem.at[ch],
            device_id=flip(half_mask), device_id_type=MESH,
        )
        copy.start()
        crossing.append(copy)
    total = jnp.zeros((rows, PAD), f32)
    for ch in range(CHUNKS):
        piece = gap(raw[:, ch * chunk : (ch + 1) * chunk], t, ch * chunk)
        for i in range(chunk // PAD):
            tile = piece[:, i * PAD : (i + 1) * PAD]
            total = total + tile * tile
    esend[...] = total

    energy = []
    for i in range(1, nt):
        copy = pltpu.make_async_remote_copy(
            esend, erecv.at[i], esend_sem.at[i], erecv_sem.at[i],
            device_id=at_tm(i), device_id_type=MESH,
        )
        copy.start()
        energy.append(copy)
    to_next = pltpu.make_async_remote_copy(
        raw.at[:, pl.ds(width - PAD, PAD)], edge.at[0], hsend_sem.at[0], hrecv_sem.at[0],
        device_id=at_tm(1), device_id_type=MESH,
    )
    to_previous = pltpu.make_async_remote_copy(
        raw.at[:, pl.ds(0, PAD)], edge.at[1], hsend_sem.at[1], hrecv_sem.at[1],
        device_id=at_tm(nt - 1), device_id_type=MESH,
    )
    to_next.start()
    to_previous.start()
    summed = lengths_ref[0]
    for i in range(1, nt):
        summed = summed + lengths_ref[i]
    count = jnp.full((1, 1), summed, jnp.int32).astype(f32)
    padded[:, :PAD] = jnp.zeros((rows, PAD), bf16)
    padded[:, PAD + width :] = jnp.zeros((rows, PAD), bf16)

    for copy in energy:
        copy.wait_recv()
    for i in range(1, nt):
        total = total + erecv[i]
    power = jnp.sum(total, axis=1, keepdims=True) / count + 1e-06
    root = jnp.sqrt(power)

    def whiten(values):
        return (values / root).astype(bf16)

    norms[0, 0] = jnp.broadcast_to(1.0 / root, (rows, PAD))

    def pass_norm(stage, mask):
        copy = pltpu.make_async_remote_copy(
            norms.at[stage, 0], norms.at[stage, 1], nsend_sem.at[stage], nrecv_sem.at[stage],
            device_id=flip(mask), device_id_type=MESH,
        )
        copy.start()
        return copy

    normed = [pass_norm(0, half_mask)]
    for ch in range(CHUNKS):
        piece = whiten(gap(raw[:, ch * chunk : (ch + 1) * chunk], t, ch * chunk))
        ext[:, PAD + ch * chunk : PAD + (ch + 1) * chunk] = piece.astype(f32)
        padded[:, PAD + ch * chunk : PAD + (ch + 1) * chunk] = piece

    to_next.wait_recv()
    to_previous.wait_recv()
    before = whiten(gap(edge[0], lax.rem(t + nt - 1, nt), width - PAD)).astype(f32)
    after = whiten(gap(edge[1], lax.rem(t + 1, nt), 0)).astype(f32)
    ext[:, :PAD] = jnp.where(t > 0, before, 0.0)
    ext[:, PAD + width :] = jnp.where(t < nt - 1, after, 0.0)

    top = FINE * (COARSE - 1) - HALF
    for pair in range(rows // 2):
        both = []
        for c in (2 * pair, 2 * pair + 1):
            row = jnp.broadcast_to(ext[c : c + 1, :], (FINE, width + 2 * PAD))
            rolled = pltpu.roll(
                row, width + 2 * PAD - (PAD - top), 1, stride=1, stride_axis=0
            )
            both.append(rolled[:, :span])
        lhs[2 * FINE * pair : 2 * FINE * (pair + 1), :] = jnp.concatenate(both, axis=0).astype(bf16)

    sends = []

    def multiply(first, last):
        for a in range(COARSE):
            offset = PAD - FINE * (COARSE - 1) + FINE * a
            rhs[a * rows : (a + 1) * rows, first:last] = padded[:, offset + first : offset + last]
        return lax.dot_general(
            lhs[:, first:last], rhs[:, first:last],
            (((1,), (1,)), ((), ())), preferred_element_type=f32,
        )

    def correlate(slot):
        scatter(slot, multiply(0, span))

    def scatter(slot, product):
        part[slot] = product.astype(bf16).reshape(nt, share * FINE, COARSE * rows)
        for i in range(1, nt):
            copy = pltpu.make_async_remote_copy(
                part.at[slot, lax.rem(t + i, nt)], parts.at[slot, i],
                psend_sem.at[slot, i], precv_sem.at[slot, i],
                device_id=at_tm(i), device_id_type=MESH,
            )
            copy.start()
            sends.append(copy)

    correlate(0)

    partners_load.wait()
    first_mask = partners_ref[0, 0]
    second_mask = partners_ref[1, 0]
    swapped = first_mask != half_mask
    other = jnp.where(swapped, first_mask, second_mask)
    crossed = other >= half_mask

    ends = [0]
    pieces = []
    stages = [[] for _ in range(bits)]

    def forward(stage, ch, piece):
        hops[stage, 0, ch] = piece
        copy = pltpu.make_async_remote_copy(
            hops.at[stage, 0, ch], hops.at[stage, 1, ch],
            bsend_sem.at[stage, ch], brecv_sem.at[stage, ch],
            device_id=flip(1 << stage), device_id_type=MESH,
        )
        copy.start()
        stages[stage].append(copy)

    def place(ch, piece):
        padded[:, PAD + ch * chunk : PAD + (ch + 1) * chunk] = piece

    for ch in range(CHUNKS):
        crossing[ch].wait_recv()
        arrived = cross[1, ch]
        forward(0, ch, jnp.where(crossed, arrived, cross[0, ch]))
        place(ch, arrived)
    normed[0].wait_recv()
    norms[1, 0] = jnp.where(crossed, norms[0, 1], norms[0, 0])
    normed.append(pass_norm(1, 1))
    correlate(1)
    for stage in range(bits):
        taken = lax.rem(other // (1 << stage), 2) == 1
        for ch in range(CHUNKS):
            stages[stage][ch].wait_recv()
            piece = jnp.where(taken, hops[stage, 1, ch], hops[stage, 0, ch])
            if stage < bits - 1:
                forward(stage + 1, ch, piece)
            else:
                place(ch, piece)
                if ch in STOPS:
                    done = ends[-1]
                    ends.append(span if ch == CHUNKS - 1 else (ch + 1) * chunk)
                    pieces.append(multiply(done, ends[-1]))
        if stage < bits - 1:
            normed[stage + 1].wait_recv()
            norms[stage + 2, 0] = jnp.where(taken, norms[stage + 1, 1], norms[stage + 1, 0])
            normed.append(pass_norm(stage + 2, 2 << stage))
    scatter(2, functools.reduce(jnp.add, pieces))

    scale = 1.0 / jnp.sqrt(count)
    full = COARSE * rows // PAD
    quad = PAD // rows
    lane = lax.broadcasted_iota(jnp.int32, (full * FINE, PAD), 1)

    def gathered(slot):
        mine = part[slot, t].astype(f32)
        for i in range(1, nt):
            sends[slot * (nt - 1) + i - 1].wait_recv()
            mine = mine + parts[slot, i].astype(f32)
        mine = mine * scale
        out = []
        for c0 in range(0, share, quad):
            blocks = []
            rests = []
            for c in range(c0, min(c0 + quad, share)):
                own = mine[c * FINE : (c + 1) * FINE]
                blocks.append(jnp.concatenate(
                    [own[:, j * PAD : (j + 1) * PAD] for j in range(full)], axis=0
                ))
                rests.append(own[:, full * PAD :])
            real = len(blocks)
            blocks += [jnp.zeros((full * FINE, PAD), f32)] * (quad - real)
            step = 1
            while step < quad:
                odd = lax.rem(lane // (rows * step), 2) == 1
                for i in range(quad):
                    if not i & step:
                        one, two = blocks[i], blocks[i + step]
                        blocks[i] = jnp.where(odd, pltpu.roll(two, rows * step, 1), one)
                        blocks[i + step] = jnp.where(odd, two, pltpu.roll(one, PAD - rows * step, 1))
                step *= 2
            lags = [
                blocks[i][j * FINE : (j + 1) * FINE] for j in range(full) for i in range(quad)
            ]
            if real < quad:
                rests.append(jnp.zeros((FINE, PAD - real * rows), f32))
            lags.append(jnp.concatenate(rests, axis=1))
            lags.append(jnp.zeros((PAD - FINE * COARSE, PAD), f32))
            turned = jnp.concatenate(lags, axis=0).T
            out.append(turned.reshape(quad, rows, PAD)[:real])
        return jnp.concatenate(out, axis=0)

    shape = (share, rows, PAD)
    index, column, lag = (lax.broadcasted_iota(jnp.int32, shape, i) for i in range(3))
    killed = (lag == HALF) & (column == t * share + index)
    out_ref[:, :rows, :] = jnp.where(killed, 0.0, gathered(0))[:, :, :LAGS]
    near = gathered(1) * norms[0, 1][None]
    normed[bits].wait_recv()
    factor = jnp.where(taken, norms[bits, 1], norms[bits, 0])
    far = gathered(2) * factor[None]
    out_ref[:, rows : 2 * rows, :] = jnp.where(swapped, far, near)[:, :, :LAGS]
    out_ref[:, 2 * rows :, :] = jnp.where(swapped, near, far)[:, :, :LAGS]

    for copy in energy + [to_next, to_previous] + crossing + sum(stages, []) + normed + sends:
        copy.wait_send()


def shards(nb, nt, traces, partners, lengths):
    rows, width = traces.shape
    share = rows // nt
    bits = nb.bit_length() - 2
    chunk = width // CHUNKS
    span = width + PAD
    f32, bf16 = jnp.float32, jnp.bfloat16
    dma = pltpu.SemaphoreType.DMA
    slots = ROUNDS + 1
    found = pl.pallas_call(
        functools.partial(kernel, nb, nt, rows, width),
        out_shape=pltpu.VMEM((share, slots * rows, LAGS), f32),
        in_specs=[
            pl.BlockSpec(memory_space=pl.ANY),
            pl.BlockSpec(memory_space=pl.ANY),
            pl.BlockSpec(memory_space=pl.ANY),
        ],
        out_specs=pl.BlockSpec(memory_space=pltpu.VMEM),
        scratch_shapes=[
            pltpu.SMEM(partners.shape, jnp.int32),
            pltpu.SMEM(lengths.shape, jnp.int32),
            dma((2,)),
            pltpu.VMEM((rows, width), f32),
            pltpu.VMEM((2, rows, PAD), f32),
            pltpu.VMEM((rows, PAD), f32),
            pltpu.VMEM((nt, rows, PAD), f32),
            pltpu.VMEM((rows, width + 2 * PAD), f32),
            pltpu.VMEM((rows * FINE, span), bf16),
            pltpu.VMEM((COARSE * rows, span), bf16),
            pltpu.VMEM((rows, width + 2 * PAD), bf16),
            pltpu.VMEM((2, CHUNKS, rows, chunk), bf16),
            pltpu.VMEM((bits, 2, CHUNKS, rows, chunk), bf16),
            pltpu.VMEM((bits + 1, 2, rows, PAD), f32),
            pltpu.VMEM((slots, nt, share * FINE, COARSE * rows), bf16),
            pltpu.VMEM((slots, nt, share * FINE, COARSE * rows), bf16),
            dma,
            dma((nt,)), dma((nt,)),
            dma((2,)), dma((2,)),
            dma((CHUNKS,)), dma((CHUNKS,)),
            dma((bits, CHUNKS)), dma((bits, CHUNKS)),
            dma((bits + 1,)), dma((bits + 1,)),
            dma((slots, nt)), dma((slots, nt)),
        ],
        compiler_params=pltpu.CompilerParams(collective_id=0, has_side_effects=True),
    )(traces, partners, lengths)
    found = found.reshape(share, slots, rows, LAGS)
    return jnp.transpose(found, (0, 3, 1, 2))


def solution(mesh):
    placed = (P("block", "tm"), P(), P())
    return jax.shard_map(
        functools.partial(shards, mesh.shape["block"], mesh.shape["tm"]),
        mesh=mesh,
        in_specs=placed,
        out_specs=P(("block", "tm"), None, None, None),
        check_vma=False,
    )
```

```python
import functools

import jax
import jax.numpy as jnp
from jax import lax
from jax.experimental import pallas as pl
from jax.experimental.pallas import tpu as pltpu
from jax.sharding import PartitionSpec as P

HALF = 50
ROUNDS = 2
LAGS = 101
FINE = 8
COARSE = 13
PAD = 128
CHUNKS = 8
STOPS = (1, 3, 5, 7)
MESH = pl.DeviceIdType.MESH


def kernel(
    nb, nt, rows, width,
    traces_ref, partners_hbm, lengths_hbm, out_ref, partners_ref, lengths_ref, table_sem,
    raw, edge, esend, erecv, ext, lhs, rhs, padded, cross, hops, norms, part, parts,
    load_sem, esend_sem, erecv_sem, hsend_sem, hrecv_sem,
    csend_sem, crecv_sem, bsend_sem, brecv_sem,
    nsend_sem, nrecv_sem, psend_sem, precv_sem,
):
    b = lax.axis_index("block")
    t = lax.axis_index("tm")
    bits = nb.bit_length() - 2
    half_mask = nb // 2
    share = rows // nt
    chunk = width // CHUNKS
    span = width + PAD
    f32, bf16 = jnp.float32, jnp.bfloat16

    def at_tm(i):
        return (b, lax.rem(t + i, nt))

    def flip(mask):
        size = 2 * mask
        low = lax.rem(b, size)
        return (b - low + lax.rem(low + mask, size), t)

    barrier = pltpu.get_barrier_semaphore()
    peers = [flip(1 << i) for i in range(bits, -1, -1)] + [at_tm(i) for i in range(1, nt)]
    for peer in peers:
        pl.semaphore_signal(barrier, inc=1, device_id=peer, device_id_type=MESH)

    load = pltpu.make_async_copy(traces_ref, raw, load_sem)
    load.start()
    lengths_load = pltpu.make_async_copy(lengths_hbm, lengths_ref, table_sem.at[0])
    partners_load = pltpu.make_async_copy(partners_hbm, partners_ref, table_sem.at[1])
    lengths_load.start()
    partners_load.start()
    def gap(values, index, first):
        length = lengths_ref[index]
        begin = length // 2
        position = first + lax.broadcasted_iota(jnp.int32, values.shape, 1)
        recorded = (position < begin) | (position >= begin + width - length)
        return jnp.where(recorded, values, 0.0)

    lengths_load.wait()
    load.wait()
    total = jnp.zeros((rows, PAD), f32)
    for ch in range(CHUNKS):
        piece = gap(raw[:, ch * chunk : (ch + 1) * chunk], t, ch * chunk)
        cross[0, ch] = piece.astype(bf16)
        for i in range(chunk // PAD):
            tile = piece[:, i * PAD : (i + 1) * PAD]
            total = total + tile * tile
    esend[...] = total
    pl.semaphore_wait(barrier, len(peers))

    energy = []
    for i in range(1, nt):
        copy = pltpu.make_async_remote_copy(
            esend, erecv.at[i], esend_sem.at[i], erecv_sem.at[i],
            device_id=at_tm(i), device_id_type=MESH,
        )
        copy.start()
        energy.append(copy)
    to_next = pltpu.make_async_remote_copy(
        raw.at[:, pl.ds(width - PAD, PAD)], edge.at[0], hsend_sem.at[0], hrecv_sem.at[0],
        device_id=at_tm(1), device_id_type=MESH,
    )
    to_previous = pltpu.make_async_remote_copy(
        raw.at[:, pl.ds(0, PAD)], edge.at[1], hsend_sem.at[1], hrecv_sem.at[1],
        device_id=at_tm(nt - 1), device_id_type=MESH,
    )
    to_next.start()
    to_previous.start()
    crossing = []
    for ch in range(CHUNKS):
        copy = pltpu.make_async_remote_copy(
            cross.at[0, ch], cross.at[1, ch], csend_sem.at[ch], crecv_sem.at[ch],
            device_id=flip(half_mask), device_id_type=MESH,
        )
        copy.start()
        crossing.append(copy)

    summed = lengths_ref[0]
    for i in range(1, nt):
        summed = summed + lengths_ref[i]
    count = jnp.full((1, 1), summed, jnp.int32).astype(f32)
    padded[:, :PAD] = jnp.zeros((rows, PAD), bf16)
    padded[:, PAD + width :] = jnp.zeros((rows, PAD), bf16)

    for copy in energy:
        copy.wait_recv()
    for i in range(1, nt):
        total = total + erecv[i]
    power = jnp.sum(total, axis=1, keepdims=True) / count + 1e-06
    root = jnp.sqrt(power)

    def whiten(values):
        return (values / root).astype(bf16)

    norms[0, 0] = jnp.broadcast_to(1.0 / root, (rows, PAD))

    def pass_norm(stage, mask):
        copy = pltpu.make_async_remote_copy(
            norms.at[stage, 0], norms.at[stage, 1], nsend_sem.at[stage], nrecv_sem.at[stage],
            device_id=flip(mask), device_id_type=MESH,
        )
        copy.start()
        return copy

    normed = [pass_norm(0, half_mask)]
    for ch in range(CHUNKS):
        piece = whiten(gap(raw[:, ch * chunk : (ch + 1) * chunk], t, ch * chunk))
        ext[:, PAD + ch * chunk : PAD + (ch + 1) * chunk] = piece.astype(f32)
        padded[:, PAD + ch * chunk : PAD + (ch + 1) * chunk] = piece

    to_next.wait_recv()
    to_previous.wait_recv()
    before = whiten(gap(edge[0], lax.rem(t + nt - 1, nt), width - PAD)).astype(f32)
    after = whiten(gap(edge[1], lax.rem(t + 1, nt), 0)).astype(f32)
    ext[:, :PAD] = jnp.where(t > 0, before, 0.0)
    ext[:, PAD + width :] = jnp.where(t < nt - 1, after, 0.0)

    top = FINE * (COARSE - 1) - HALF
    for pair in range(rows // 2):
        both = []
        for c in (2 * pair, 2 * pair + 1):
            row = jnp.broadcast_to(ext[c : c + 1, :], (FINE, width + 2 * PAD))
            rolled = pltpu.roll(
                row, width + 2 * PAD - (PAD - top), 1, stride=1, stride_axis=0
            )
            both.append(rolled[:, :span])
        lhs[2 * FINE * pair : 2 * FINE * (pair + 1), :] = jnp.concatenate(both, axis=0).astype(bf16)

    sends = []

    def multiply(first, last):
        for a in range(COARSE):
            offset = PAD - FINE * (COARSE - 1) + FINE * a
            rhs[a * rows : (a + 1) * rows, first:last] = padded[:, offset + first : offset + last]
        return lax.dot_general(
            lhs[:, first:last], rhs[:, first:last],
            (((1,), (1,)), ((), ())), preferred_element_type=f32,
        )

    def correlate(slot):
        scatter(slot, multiply(0, span))

    def scatter(slot, product):
        part[slot] = product.astype(bf16).reshape(nt, share * FINE, COARSE * rows)
        for i in range(1, nt):
            copy = pltpu.make_async_remote_copy(
                part.at[slot, lax.rem(t + i, nt)], parts.at[slot, i],
                psend_sem.at[slot, i], precv_sem.at[slot, i],
                device_id=at_tm(i), device_id_type=MESH,
            )
            copy.start()
            sends.append(copy)

    correlate(0)

    partners_load.wait()
    first_mask = partners_ref[0, 0]
    second_mask = partners_ref[1, 0]
    swapped = first_mask != half_mask
    other = jnp.where(swapped, first_mask, second_mask)
    crossed = other >= half_mask

    ends = [0]
    pieces = []
    stages = [[] for _ in range(bits)]

    def forward(stage, ch, piece):
        hops[stage, 0, ch] = piece
        copy = pltpu.make_async_remote_copy(
            hops.at[stage, 0, ch], hops.at[stage, 1, ch],
            bsend_sem.at[stage, ch], brecv_sem.at[stage, ch],
            device_id=flip(1 << stage), device_id_type=MESH,
        )
        copy.start()
        stages[stage].append(copy)

    def place(ch, piece):
        padded[:, PAD + ch * chunk : PAD + (ch + 1) * chunk] = piece

    for ch in range(CHUNKS):
        crossing[ch].wait_recv()
        arrived = cross[1, ch]
        forward(0, ch, jnp.where(crossed, arrived, cross[0, ch]))
        place(ch, arrived)
    normed[0].wait_recv()
    norms[1, 0] = jnp.where(crossed, norms[0, 1], norms[0, 0])
    normed.append(pass_norm(1, 1))
    correlate(1)
    for stage in range(bits):
        taken = lax.rem(other // (1 << stage), 2) == 1
        for ch in range(CHUNKS):
            stages[stage][ch].wait_recv()
            piece = jnp.where(taken, hops[stage, 1, ch], hops[stage, 0, ch])
            if stage < bits - 1:
                forward(stage + 1, ch, piece)
            else:
                place(ch, piece)
                if ch in STOPS:
                    done = ends[-1]
                    ends.append(span if ch == CHUNKS - 1 else (ch + 1) * chunk)
                    pieces.append(multiply(done, ends[-1]))
        if stage < bits - 1:
            normed[stage + 1].wait_recv()
            norms[stage + 2, 0] = jnp.where(taken, norms[stage + 1, 1], norms[stage + 1, 0])
            normed.append(pass_norm(stage + 2, 2 << stage))
    scatter(2, functools.reduce(jnp.add, pieces))

    scale = 1.0 / jnp.sqrt(count)
    full = COARSE * rows // PAD
    quad = PAD // rows
    lane = lax.broadcasted_iota(jnp.int32, (full * FINE, PAD), 1)

    def gathered(slot):
        mine = part[slot, t].astype(f32)
        for i in range(1, nt):
            sends[slot * (nt - 1) + i - 1].wait_recv()
            mine = mine + parts[slot, i].astype(f32)
        out = []
        for c0 in range(0, share, quad):
            blocks = []
            rests = []
            for c in range(c0, min(c0 + quad, share)):
                own = mine[c * FINE : (c + 1) * FINE]
                blocks.append(jnp.concatenate(
                    [own[:, j * PAD : (j + 1) * PAD] for j in range(full)], axis=0
                ))
                rests.append(own[:, full * PAD :])
            real = len(blocks)
            blocks += [jnp.zeros((full * FINE, PAD), f32)] * (quad - real)
            step = 1
            while step < quad:
                odd = lax.rem(lane // (rows * step), 2) == 1
                for i in range(quad):
                    if not i & step:
                        one, two = blocks[i], blocks[i + step]
                        blocks[i] = jnp.where(odd, pltpu.roll(two, rows * step, 1), one)
                        blocks[i + step] = jnp.where(odd, two, pltpu.roll(one, PAD - rows * step, 1))
                step *= 2
            lags = [
                blocks[i][j * FINE : (j + 1) * FINE] for j in range(full) for i in range(quad)
            ]
            if real < quad:
                rests.append(jnp.zeros((FINE, PAD - real * rows), f32))
            lags.append(jnp.concatenate(rests, axis=1))
            lags.append(jnp.zeros((PAD - FINE * COARSE, PAD), f32))
            turned = jnp.concatenate(lags, axis=0).T
            out.append(turned.reshape(quad, rows, PAD)[:real])
        return jnp.concatenate(out, axis=0)

    shape = (share, rows, PAD)
    index, column, lag = (lax.broadcasted_iota(jnp.int32, shape, i) for i in range(3))
    killed = (lag == HALF) & (column == t * share + index)
    out_ref[:, :rows, :] = jnp.where(killed, 0.0, gathered(0) * scale)[:, :, :LAGS]
    near = gathered(1) * (norms[0, 1] * scale)[None]
    normed[bits].wait_recv()
    factor = jnp.where(taken, norms[bits, 1], norms[bits, 0])
    far = gathered(2) * (factor * scale)[None]
    out_ref[:, rows : 2 * rows, :] = jnp.where(swapped, far, near)[:, :, :LAGS]
    out_ref[:, 2 * rows :, :] = jnp.where(swapped, near, far)[:, :, :LAGS]

    for copy in energy + [to_next, to_previous] + crossing + sum(stages, []) + normed + sends:
        copy.wait_send()


def shards(nb, nt, traces, partners, lengths):
    rows, width = traces.shape
    share = rows // nt
    bits = nb.bit_length() - 2
    chunk = width // CHUNKS
    span = width + PAD
    f32, bf16 = jnp.float32, jnp.bfloat16
    dma = pltpu.SemaphoreType.DMA
    slots = ROUNDS + 1
    found = pl.pallas_call(
        functools.partial(kernel, nb, nt, rows, width),
        out_shape=pltpu.VMEM((share, slots * rows, LAGS), f32),
        in_specs=[
            pl.BlockSpec(memory_space=pl.ANY),
            pl.BlockSpec(memory_space=pl.ANY),
            pl.BlockSpec(memory_space=pl.ANY),
        ],
        out_specs=pl.BlockSpec(memory_space=pltpu.VMEM),
        scratch_shapes=[
            pltpu.SMEM(partners.shape, jnp.int32),
            pltpu.SMEM(lengths.shape, jnp.int32),
            dma((2,)),
            pltpu.VMEM((rows, width), f32),
            pltpu.VMEM((2, rows, PAD), f32),
            pltpu.VMEM((rows, PAD), f32),
            pltpu.VMEM((nt, rows, PAD), f32),
            pltpu.VMEM((rows, width + 2 * PAD), f32),
            pltpu.VMEM((rows * FINE, span), bf16),
            pltpu.VMEM((COARSE * rows, span), bf16),
            pltpu.VMEM((rows, width + 2 * PAD), bf16),
            pltpu.VMEM((2, CHUNKS, rows, chunk), bf16),
            pltpu.VMEM((bits, 2, CHUNKS, rows, chunk), bf16),
            pltpu.VMEM((bits + 1, 2, rows, PAD), f32),
            pltpu.VMEM((slots, nt, share * FINE, COARSE * rows), bf16),
            pltpu.VMEM((slots, nt, share * FINE, COARSE * rows), bf16),
            dma,
            dma((nt,)), dma((nt,)),
            dma((2,)), dma((2,)),
            dma((CHUNKS,)), dma((CHUNKS,)),
            dma((bits, CHUNKS)), dma((bits, CHUNKS)),
            dma((bits + 1,)), dma((bits + 1,)),
            dma((slots, nt)), dma((slots, nt)),
        ],
        compiler_params=pltpu.CompilerParams(collective_id=0, has_side_effects=True),
    )(traces, partners, lengths)
    found = found.reshape(share, slots, rows, LAGS)
    return jnp.transpose(found, (0, 3, 1, 2))


def solution(mesh):
    placed = (P("block", "tm"), P(), P())
    return jax.shard_map(
        functools.partial(shards, mesh.shape["block"], mesh.shape["tm"]),
        mesh=mesh,
        in_specs=placed,
        out_specs=P(("block", "tm"), None, None, None),
        check_vma=False,
    )
```
